128 devices in a mesh: ctx: 8 (over x_hi, y), tile: 16 (over z, x_lo, core).
Axes of the slice: x: 4 (x_hi: 2, x_lo: 2; x = x_hi * 2 + x_lo), y: 4, z: 4, core: 2. Of those that a mesh axis runs over, the one named last changes fastest.
Arguments:
- syndrome_bits: int32 [8, 2, 64, 512], P(None, None, 'ctx', 'tile'), may hold values from 0 to 1
- region_assign: int32 [32, 256], P('ctx', 'tile'), may hold values from 0 to 127
- state_in: bfloat16 [64, 512, 512], P('ctx', 'tile'), may hold values from -3 to 3
- bit_to_candidate: float32 [2, 512], replicated, may hold values from -5 to 5
- bit_to_gate: float32 [2, 512], replicated, may hold values from -5 to 5
- conv_weight: bfloat16 [9, 512, 512], replicated, may hold values from -0.09375 to 0.09375
- gate_weight: bfloat16 [512, 512], replicated, may hold values from -0.25 to 0.25
- gate_bias: float32 [512], replicated, may hold values from -4 to 1
- pool_weight: bfloat16 [512, 1024], replicated, may hold values from -0.25 to 0.25
- region_embed: bfloat16 [1024, 1024], P('ctx'), may hold values from -6 to 6
- attn_norm_gain: float32 [1024], replicated, may hold values from 0.1 to 1.9
- query_weight: bfloat16 [1024, 1024], replicated
- key_weight: bfloat16 [1024, 1024], replicated
- value_weight: bfloat16 [1024, 1024], replicated, may hold values from -0.1875 to 0.1875
- out_weight: bfloat16 [1024, 1024], replicated, may hold values from -0.1875 to 0.1875
- mlp_norm_gain: float32 [1024], replicated, may hold values from 0.1 to 1.9
- mlp_up: bfloat16 [1024, 2048], replicated, may hold values from -0.1875 to 0.1875
- mlp_down: bfloat16 [2048, 1024], replicated, may hold values from -0.125 to 0.125
- return_weight: bfloat16 [1024, 512], replicated, may hold values from -0.1875 to 0.1875
Outputs:
- state_out: bfloat16 [64, 512, 512], P('ctx', 'tile')
- context_out: bfloat16 [1024, 1024], P('ctx')
The draws below stay inside these ranges and needn't reach their ends.
All inputs are finite; a program needn't handle non-finite values.
Results may differ from the reference program's by a relative error of at most 0.02.
Values may be sent and summed in bfloat16 or wider, within the bound.
A program may use at most 128 MiB of HBM per device.

```python
import math
import jax
import jax.numpy as jnp
from jax import lax

C = 512
E = 1024
HEADS = 8
HDIM = 128
MLP = 2048
ROUNDS = 8
PR = 8
REG_DEV = 128
NR = 64
NC = 512
REGIONS = 1024


def shared_query(key):
    return jax.random.normal(jax.random.fold_in(key, 11), (E, E), jnp.float32) * E ** (-0.5)


def draw_query_weight(key, part):
    return shared_query(key).astype(jnp.bfloat16)


def draw_key_weight(key, part):
    fresh = jax.random.normal(jax.random.fold_in(key, 13), (E, E), jnp.float32) * E ** (-0.5)
    return fresh.astype(jnp.bfloat16)


def with_ends(values, rng, smallest, top_value):
    spot = [jax.random.randint(jax.random.fold_in(rng, axis), (), 0, length) for axis, length in enumerate(values.shape)]
    longest = values.shape.index(max(values.shape))
    next_to = spot[:longest] + [(spot[longest] + 1) % values.shape[longest]] + spot[longest + 1:]
    return values.at[tuple(spot)].set(smallest).at[tuple(next_to)].set(top_value)


def levels(stream_key, extent, split, least, top_value):
    def one(position, shards_of):
        draws = jax.random.uniform(jax.random.fold_in(jax.random.fold_in(stream_key, 6), position), (shards_of,), jnp.float32, least / len(split), top_value / len(split))
        return jnp.repeat(jnp.exp(draws), extent[position] // shards_of).reshape((-1,) + (1,) * (len(extent) - position - 1))

    level = one(*split[0])
    for cut in split[1:]:
        level = level * one(*cut)
    return level


def noise(key, shape, spread, most, pieces=(), held_as=jnp.bfloat16):
    drawn = jax.random.normal(key, shape, jnp.float32) * spread
    if len(pieces) > 0:
        drawn = levels(key, shape, pieces, -0.22, 0.18) * drawn
    return jnp.clip(drawn, min=-most, max=most).astype(held_as)


def setup_inputs(seed: int = 0) -> dict:
    key_of = jax.random.split(jax.random.key(seed), 20)
    syndrome_bits = with_ends(jax.random.randint(key_of[0], (ROUNDS, 2, NR, NC), 0, 2), jax.random.fold_in(key_of[0], 1), 0, 1).astype(jnp.int32)
    region_assign = with_ends(jax.random.randint(key_of[1], (NR // 2, NC // 2), 0, REG_DEV), jax.random.fold_in(key_of[1], 1), 0, REG_DEV - 1).astype(jnp.int32)
    state_in = noise(key_of[2], (NR, NC, C), 0.5, 3.0, ((0, 8), (1, 16)))
    bit_to_candidate = noise(key_of[3], (2, C), 1.0, 5.0, (), jnp.float32)
    bit_to_gate = noise(key_of[4], (2, C), 1.0, 5.0, (), jnp.float32)
    conv_weight = noise(key_of[5], (9, C, C), (9 * C) ** -0.5, 0.09375)
    gate_weight = noise(key_of[6], (C, C), C ** -0.5, 0.25)
    gate_bias = jnp.clip(jax.random.uniform(key_of[7], (C,), jnp.float32, -4.0, 1.0), -4.0, 1.0)
    pool_weight = noise(key_of[8], (C, E), C ** -0.5, 0.25)
    region_embed = noise(key_of[9], (REGIONS, E), 1.0, 6.0, ((0, 8),))
    attn_norm_gain = jnp.clip(1.0 + 0.18 * jax.random.normal(key_of[10], (E,), jnp.float32), 0.1, 1.9)
    query_weight = draw_query_weight(jax.random.fold_in(key_of[19], 71), 0)
    key_weight = draw_key_weight(jax.random.fold_in(key_of[19], 71), 0)
    value_weight = noise(key_of[13], (E, E), E ** -0.5, 0.1875)
    out_weight = noise(key_of[14], (E, E), E ** -0.5, 0.1875)
    mlp_norm_gain = jnp.clip(1.0 + 0.18 * jax.random.normal(key_of[15], (E,), jnp.float32), 0.1, 1.9)
    mlp_up = noise(key_of[16], (E, MLP), E ** -0.5, 0.1875)
    mlp_down = noise(key_of[17], (MLP, E), MLP ** -0.5, 0.125)
    return_weight = noise(key_of[18], (E, C), E ** -0.5, 0.1875)
    return dict(syndrome_bits=syndrome_bits, region_assign=region_assign, state_in=state_in, bit_to_candidate=bit_to_candidate, bit_to_gate=bit_to_gate, conv_weight=conv_weight, gate_weight=gate_weight, gate_bias=gate_bias, pool_weight=pool_weight, region_embed=region_embed, attn_norm_gain=attn_norm_gain, query_weight=query_weight, key_weight=key_weight, value_weight=value_weight, out_weight=out_weight, mlp_norm_gain=mlp_norm_gain, mlp_up=mlp_up, mlp_down=mlp_down, return_weight=return_weight)


def product(left, right):
    return jnp.dot(left.astype(jnp.float32), right.astype(jnp.float32), precision=lax.Precision.HIGHEST)

def rms_norm(values, gain):
    return values * lax.rsqrt(lax.optimization_barrier(jnp.mean(values * values, axis=-1, keepdims=True)) + 1e-05) * gain

def advance(state, syndrome_now, conv_weight, gate_weight, gate_bias, bit_to_candidate, bit_to_gate):
    patch_rows, patch_cols, channels = state.shape
    rounded = state.astype(jnp.bfloat16)
    padded = jnp.pad(rounded, ((1, 1), (1, 1), (0, 0)))
    columns = jnp.concatenate([padded[offset_row:offset_row + patch_rows, offset_col:offset_col + patch_cols] for offset_row in range(3) for offset_col in range(3)], axis=-1)
    syndrome_flags = syndrome_now.astype(jnp.float32)
    drive_cand = syndrome_flags[0][..., None] * bit_to_candidate[0] + syndrome_flags[1][..., None] * bit_to_candidate[1]
    drive_gate = syndrome_flags[0][..., None] * bit_to_gate[0] + syndrome_flags[1][..., None] * bit_to_gate[1]
    candidate = product(columns.reshape(patch_rows * patch_cols, 9 * channels), conv_weight.reshape(9 * channels, channels)).reshape(patch_rows, patch_cols, channels) + drive_cand
    update_gate = jax.nn.sigmoid(product(rounded.reshape(patch_rows * patch_cols, channels), gate_weight).reshape(patch_rows, patch_cols, channels) + drive_gate + gate_bias)
    return state + update_gate * (jnp.tanh(candidate) - state)

def reference(syndrome_bits, region_assign, state_in, bit_to_candidate, bit_to_gate, conv_weight, gate_weight, gate_bias, pool_weight, region_embed, attn_norm_gain, query_weight, key_weight, value_weight, out_weight, mlp_norm_gain, mlp_up, mlp_down, return_weight):
    state = state_in.astype(jnp.float32)
    patch_rows, patch_cols, channels = state.shape
    context_out = None
    for round_index in range(ROUNDS):
        if round_index == ROUNDS // 2:
            pooled = state.reshape(patch_rows // 2, 2, patch_cols // 2, 2, channels).mean(axis=(1, 3)).astype(jnp.bfloat16)
            projected = product(pooled.reshape(-1, channels), pool_weight)
            band = (jnp.arange(patch_rows // 2, dtype=jnp.int32) // (PR // 2))[:, None]
            token_index = (band * REG_DEV + region_assign).astype(jnp.int32).reshape(-1)
            tokens = region_embed.astype(jnp.float32) + jax.ops.segment_sum(projected, token_index, num_segments=REGIONS)
            token_count = tokens.shape[0]
            normed = rms_norm(tokens, attn_norm_gain).astype(jnp.bfloat16)
            queries = product(normed, query_weight).astype(jnp.bfloat16)
            key_rows = product(normed, key_weight).astype(jnp.bfloat16)
            value_rows = product(normed, value_weight).astype(jnp.bfloat16)
            query_heads = queries.astype(jnp.float32).reshape(token_count, HEADS, HDIM).transpose(1, 0, 2)
            key_heads = key_rows.astype(jnp.float32).reshape(token_count, HEADS, HDIM).transpose(1, 0, 2)
            value_heads = value_rows.astype(jnp.float32).reshape(token_count, HEADS, HDIM).transpose(1, 0, 2)
            scores = jnp.einsum('hqd,hkd->hqk', query_heads, key_heads, precision=lax.Precision.HIGHEST) / math.sqrt(HDIM)
            running_max = lax.optimization_barrier(jnp.max(scores, axis=-1, keepdims=True))
            weights = jnp.exp(scores - running_max)
            denominator = lax.optimization_barrier(jnp.sum(weights, axis=-1))
            weights_low = lax.optimization_barrier(weights.astype(jnp.bfloat16)).astype(jnp.float32)
            weighted = jnp.einsum('hqk,hkd->hqd', weights_low, value_heads, precision=lax.Precision.HIGHEST) / denominator[..., None]
            attention = weighted.transpose(1, 0, 2).reshape(token_count, HEADS * HDIM).astype(jnp.bfloat16)
            attended = tokens + product(attention, out_weight)
            hidden = jax.nn.gelu(product(rms_norm(attended, mlp_norm_gain).astype(jnp.bfloat16), mlp_up)).astype(jnp.bfloat16)
            context_out = (attended + product(hidden, mlp_down)).astype(jnp.bfloat16)
            returned = product(context_out, return_weight)
            share_back = returned[token_index].reshape(patch_rows // 2, patch_cols // 2, channels)
            state = (state.reshape(patch_rows // 2, 2, patch_cols // 2, 2, channels) + share_back[:, None, :, None, :]).reshape(patch_rows, patch_cols, channels)
        state = advance(state, syndrome_bits[round_index], conv_weight, gate_weight, gate_bias, bit_to_candidate, bit_to_gate)
    return (state.astype(jnp.bfloat16), context_out)
```

```python
import functools
import math

import jax
import jax.numpy as jnp
from jax import lax
from jax.experimental import pallas as pl
from jax.experimental.pallas import tpu as pltpu
from jax.sharding import PartitionSpec as P

MESH = pl.DeviceIdType.MESH
BF16 = jnp.bfloat16
F32 = jnp.float32

HEADS = 8
HDIM = 128
ROUNDS = 8
HALF = 4
C = 512
E = 1024
ROWS = 16
COLS = 48
OWN_ROWS = slice(4, 12)
LANES = 128
ASSIGN = 40

MOVES = ((-1, 0), (1, 0), (0, -1), (0, 1), (-1, -1), (-1, 1), (1, -1), (1, 1))


def dot(left, right):
    return jnp.dot(left, right, preferred_element_type=F32)


def rms_norm(values, gain):
    return values * lax.rsqrt(jnp.mean(values * values, axis=-1, keepdims=True) + 1e-05) * gain


def window(
    extra_in,
    state_in,
    bit_to_candidate,
    bit_to_gate,
    conv_weight,
    gate_weight,
    gate_bias,
    pool_weight,
    region_embed,
    attn_norm_gain,
    query_weight,
    key_weight,
    value_weight,
    out_weight,
    mlp_norm_gain,
    mlp_up,
    mlp_down,
    return_weight,
    state_out,
    context_out,
    state,
    taps,
    extra,
    extra_low,
    drive,
    conv_w,
    gate_w,
    pool_w,
    embed_w,
    qkv_w,
    out_w,
    up_w,
    down_w,
    return_w,
    edge_ns,
    edge_ew,
    extra_ns,
    extra_ew,
    halo_ns,
    halo_ew,
    halo_corner,
    halo_extra_ns,
    halo_extra_ew,
    halo_extra_corner,
    partial_send,
    partial_recv,
    summed_all,
    queries,
    keys_values,
    attention_all,
    attention_full,
    weight_sem,
    edge_sem,
    halo_send,
    halo_recv,
    tile_send,
    tile_recv,
    ctx_send,
    ctx_recv,
):
    g, t = lax.axis_index("ctx"), lax.axis_index("tile")
    ctx_size, tile_size = 8, 16
    head, part = t // 2, lax.rem(t, 2)

    head_cols = pl.ds(pl.multiple_of(head * HDIM, HDIM), HDIM)
    edge_copies = [
        pltpu.make_async_copy(state_in, edge_ns.at[0], edge_sem.at[0]),
        pltpu.make_async_copy(state_in.at[:, 0:8], edge_ew.at[0, 0], edge_sem.at[1]),
        pltpu.make_async_copy(state_in.at[:, 24:32], edge_ew.at[0, 1], edge_sem.at[2]),
        pltpu.make_async_copy(extra_in, extra_ns, edge_sem.at[3]),
        pltpu.make_async_copy(extra_in.at[:, 0:8], extra_ew.at[0], edge_sem.at[4]),
        pltpu.make_async_copy(extra_in.at[:, 24:32], extra_ew.at[1], edge_sem.at[5]),
    ]
    weight_copies = [
        pltpu.make_async_copy(src, dst, weight_sem.at[i])
        for i, (src, dst) in enumerate(
            (
                (conv_weight, conv_w),
                (gate_weight, gate_w),
                (pool_weight, pool_w),
                (region_embed, embed_w),
                (query_weight.at[:, head_cols], qkv_w.at[0]),
                (key_weight.at[:, head_cols], qkv_w.at[1]),
                (value_weight.at[:, head_cols], qkv_w.at[2]),
                (out_weight, out_w),
                (mlp_up, up_w),
                (mlp_down, down_w),
                (return_weight, return_w),
            )
        )
    ]
    for copy in edge_copies:
        copy.start()
    for copy in weight_copies:
        copy.start()

    def inside(move, sign):
        dg, dt = move
        peer_g, peer_t = g + sign * dg, t + sign * dt
        return (peer_g >= 0) & (peer_g < ctx_size) & (peer_t >= 0) & (peer_t < tile_size)

    barrier = pltpu.get_barrier_semaphore()
    heard = jnp.int32(0)
    for move in MOVES[4:]:
        @pl.when(inside(move, 1))
        def _(move=move):
            pl.semaphore_signal(
                barrier, 1, device_id=(g + move[0], t + move[1]), device_id_type=MESH
            )
        heard += inside(move, -1).astype(jnp.int32)
    for step in range(1, ctx_size):
        pl.semaphore_signal(
            barrier, 1, device_id=(lax.rem(g + step, ctx_size), t), device_id_type=MESH
        )
    for step in range(1, tile_size):
        pl.semaphore_signal(
            barrier, 1, device_id=(g, lax.rem(t + step, tile_size)), device_id_type=MESH
        )

    state[...] = jnp.zeros_like(state)
    extra[...] = jnp.zeros_like(extra)

    lane_row = lax.broadcasted_iota(jnp.int32, (LANES, 2 * C), 0)
    both = jnp.concatenate([bit_to_candidate[...], bit_to_gate[...]], axis=1)
    bias = jnp.concatenate([jnp.zeros_like(gate_bias[...]), gate_bias[...]], axis=1)
    both_high = both.astype(BF16).astype(F32)
    both_low = both - both_high
    bias_high = bias.astype(BF16).astype(F32)
    bias_low = bias - bias_high
    even = lax.rem(lane_row, 2) == 0
    drive[...] = jnp.where(
        lane_row < 16,
        jnp.where(even, both_high[0:1], both_high[1:2]),
        jnp.where(
            lane_row < 32,
            jnp.where(even, both_low[0:1], both_low[1:2]),
            jnp.where(
                lane_row == 32, bias_high, jnp.where(lane_row == 33, bias_low, 0.0)
            ),
        ),
    )

    column = lax.broadcasted_iota(jnp.int32, (COLS, 1), 0)
    column_inside = ~(
        ((t == 0) & (column >= 40))
        | ((t == tile_size - 1) & (column >= 32) & (column < 40))
    )

    pl.semaphore_wait(barrier, heard + (ctx_size - 1) + (tile_size - 1))

    def halo_parts(move, half):
        dg, dt = move
        index = MOVES.index(move)
        rows = {0: slice(0, 8), -1: slice(0, 4), 1: slice(4, 8)}[dg]
        side = 0 if dt == -1 else 1
        if dt == 0:
            source, target = edge_ns.at[half, rows], halo_ns.at[half, index]
            more, more_target = extra_ns.at[rows], halo_extra_ns.at[index]
        elif dg == 0:
            source, target = edge_ew.at[half, side], halo_ew.at[half, side]
            more, more_target = extra_ew.at[side], halo_extra_ew.at[side]
        else:
            source, target = edge_ew.at[half, side, rows], halo_corner.at[half, index - 4]
            more, more_target = extra_ew.at[side, rows], halo_extra_corner.at[index - 4]
        return source, target, more, more_target

    def halo_copy(move, half):
        source, target, _, _ = halo_parts(move, half)
        index = MOVES.index(move)
        return pltpu.make_async_remote_copy(
            src_ref=source,
            dst_ref=target,
            send_sem=halo_send.at[half, index],
            recv_sem=halo_recv.at[half, index],
            device_id=(g + move[0], t + move[1]),
            device_id_type=MESH,
        )

    def extra_copy(move):
        _, _, source, target = halo_parts(move, 0)
        index = MOVES.index(move)
        return pltpu.make_async_remote_copy(
            src_ref=source,
            dst_ref=target,
            send_sem=halo_send.at[2, index],
            recv_sem=halo_recv.at[2, index],
            device_id=(g + move[0], t + move[1]),
            device_id_type=MESH,
        )

    def place(move):
        dg, dt = move
        rows = {0: slice(4, 12), -1: slice(12, 16), 1: slice(0, 4)}[dg]
        cols = {0: slice(0, 32), -1: slice(32, 40), 1: slice(40, 48)}[dt]
        return rows, cols

    def exchange(half, first):
        for move in MOVES:
            @pl.when(inside(move, 1))
            def _(move=move):
                halo_copy(move, half).start()
                if first:
                    extra_copy(move).start()
        if first:
            state[OWN_ROWS, 0:32] = edge_ns[0].astype(F32)
            extra[OWN_ROWS, 0:32] = extra_ns[...].astype(F32)
        for move in MOVES:
            @pl.when(inside(move, -1))
            def _(move=move):
                rows, cols = place(move)
                copy = halo_copy(move, half)
                copy.wait_recv()
                _, target, _, more_target = halo_parts(move, half)
                state[rows, cols] = target[...].astype(F32)
                if first:
                    extra_copy(move).wait_recv()
                    extra[rows, cols] = more_target[...].astype(F32)

    def drain(half, first):
        for move in MOVES:
            @pl.when(inside(move, 1))
            def _(move=move):
                halo_copy(move, half).wait_send()
                if first:
                    extra_copy(move).wait_send()

    def advance(half, r):
        for i in range(r, ROWS - r):
            row = state[i]
            taps[i, :, 0:C] = pltpu.roll(row, 1, 0).astype(BF16)
            taps[i, :, C : 2 * C] = row.astype(BF16)
            taps[i, :, 2 * C : 3 * C] = pltpu.roll(row, COLS - 1, 0).astype(BF16)
        round_index = half * HALF + r
        lane = lax.broadcasted_iota(jnp.int32, (LANES, 2 * C), 0)
        chosen = ((lane < 32) & (lax.rem(lane, 16) // 2 == round_index)) | (lane >= 32)
        drive_now = jnp.where(chosen, drive[...], 0.0).astype(BF16)
        low, high = r + 1, ROWS - 1 - r
        width = COLS if r < HALF - 1 else 32
        count = (high - low) * width
        candidate = dot(
            extra_low[low:high, 0:width].reshape(count, LANES), drive_now[:, 0:C]
        )
        for a in range(3):
            candidate += dot(
                taps[low + a - 1 : high + a - 1, 0:width].reshape(count, 3 * C),
                conv_w[3 * a : 3 * a + 3].reshape(3 * C, C),
            )
        gate = dot(
            taps[low:high, 0:width, C : 2 * C].reshape(count, C), gate_w[...]
        ) + dot(extra_low[low:high, 0:width].reshape(count, LANES), drive_now[:, C : 2 * C])
        update = 0.5 + 0.5 * jnp.tanh(0.5 * gate)
        before = state[low:high, 0:width].reshape(count, C)
        after = before + update * (jnp.tanh(candidate) - before)
        after = after.reshape(high - low, width, C)
        if r == HALF - 1:
            state[low:high, 0:width] = after
        else:
            for i in range(low, high):
                keep = column_inside
                if i < 4:
                    keep = keep & (g > 0)
                if i >= 12:
                    keep = keep & (g < ctx_size - 1)
                state[i] = jnp.where(keep, after[i - low], 0.0)

    def tile_copy(phase, step, source, target):
        return pltpu.make_async_remote_copy(
            src_ref=source,
            dst_ref=target,
            send_sem=tile_send.at[phase, step],
            recv_sem=tile_recv.at[phase, step],
            device_id=(g, lax.rem(t + step, tile_size)),
            device_id_type=MESH,
        )

    def ctx_copy(step, source, target):
        return pltpu.make_async_remote_copy(
            src_ref=source,
            dst_ref=target,
            send_sem=ctx_send.at[step],
            recv_sem=ctx_recv.at[step],
            device_id=(lax.rem(g + step, ctx_size), t),
            device_id_type=MESH,
        )

    def context():
        pooled = []
        for i in range(4, 12, 2):
            pair = state[i, 0:32] + state[i + 1, 0:32]
            pooled.append(((pair + pltpu.roll(pair, 31, 0)) * 0.25).astype(BF16))
        pooled = jnp.concatenate(pooled, axis=0)
        assign = jnp.concatenate(
            [extra[i, 0:32, ASSIGN : ASSIGN + 1] for i in range(4, 12, 2)], axis=0
        )
        even = lax.rem(lax.broadcasted_iota(jnp.int32, (128, 128), 0), 2) == 0
        token = lax.broadcasted_iota(jnp.int32, (128, 128), 1).astype(F32)
        member = ((assign == token) & even).astype(F32).astype(BF16)
        partial = lax.dot_general(
            member, pooled, (((0,), (0,)), ((), ())), preferred_element_type=F32
        )
        partial_send[...] = partial.reshape(tile_size, 8, C).astype(BF16)
        partial_recv[0] = partial_send[t]
        for step in range(1, tile_size):
            tile_copy(
                0, step, partial_send.at[lax.rem(t + step, tile_size)], partial_recv.at[step]
            ).start()
        total = partial_recv[0].astype(F32)
        for step in range(1, tile_size):
            tile_copy(0, step, partial_send.at[0], partial_recv.at[step]).wait_recv()
            total += partial_recv[step].astype(F32)
        summed_all[t] = total.astype(BF16)
        for step in range(1, tile_size):
            tile_copy(1, step, summed_all.at[t], summed_all.at[t]).start()
        for step in range(1, tile_size):
            sender = lax.rem(t + tile_size - step, tile_size)
            tile_copy(1, step, summed_all.at[t], summed_all.at[sender]).wait_recv()
        for copy in weight_copies[2:7]:
            copy.wait()
        summed = summed_all[...].reshape(128, C)
        tokens = embed_w[...].astype(F32) + dot(summed, pool_w[...])
        normed = rms_norm(tokens, attn_norm_gain[...]).astype(BF16)
        queries[...] = dot(normed, qkv_w[0])
        keys_values[g, 0] = dot(normed, qkv_w[1]).astype(BF16)
        keys_values[g, 1] = dot(normed, qkv_w[2]).astype(BF16)
        for step in range(1, ctx_size):
            ctx_copy(step, keys_values.at[g], keys_values.at[g]).start()
        for step in range(1, ctx_size):
            sender = lax.rem(g + ctx_size - step, ctx_size)
            ctx_copy(step, keys_values.at[g], keys_values.at[sender]).wait_recv()
        query = queries[pl.ds(pl.multiple_of(part * 64, 64), 64)].astype(BF16)
        scores = jnp.concatenate(
            [
                lax.dot_general(
                    query,
                    keys_values[i, 0],
                    (((1,), (1,)), ((), ())),
                    preferred_element_type=F32,
                )
                for i in range(ctx_size)
            ],
            axis=1,
        ) * (1.0 / math.sqrt(HDIM))
        weights = jnp.exp(scores - jnp.max(scores, axis=-1, keepdims=True))
        denominator = jnp.sum(weights, axis=-1, keepdims=True)
        weights_low = weights.astype(BF16)
        weighted = jnp.zeros((64, HDIM), F32)
        for i in range(ctx_size):
            weighted += dot(weights_low[:, i * 128 : (i + 1) * 128], keys_values[i, 1])
        attention_all[t] = (weighted / denominator).astype(BF16)
        for step in range(1, tile_size):
            tile_copy(2, step, attention_all.at[t], attention_all.at[t]).start()
        for step in range(1, tile_size):
            sender = lax.rem(t + tile_size - step, tile_size)
            tile_copy(2, step, attention_all.at[t], attention_all.at[sender]).wait_recv()
        for i in range(tile_size):
            attention_full[
                (i % 2) * 64 : (i % 2) * 64 + 64, (i // 2) * HDIM : (i // 2 + 1) * HDIM
            ] = attention_all[i]
        for copy in weight_copies[7:]:
            copy.wait()
        attended = tokens + dot(attention_full[...], out_w[...])
        mlp_in = rms_norm(attended, mlp_norm_gain[...]).astype(BF16)
        hidden = jax.nn.gelu(dot(mlp_in, up_w[...])).astype(BF16)
        context = (attended + dot(hidden, down_w[...])).astype(BF16)
        context_out[...] = context
        returned = dot(context, return_w[...])
        returned_high = returned.astype(BF16)
        returned_low = (returned - returned_high.astype(F32)).astype(BF16)
        assign = extra[OWN_ROWS, 0:32, ASSIGN : ASSIGN + 1].reshape(256, 1)
        member = (
            (assign == lax.broadcasted_iota(jnp.int32, (256, 128), 1).astype(F32))
            .astype(F32)
            .astype(BF16)
        )
        share = dot(member, returned_high) + dot(member, returned_low)
        after = state[OWN_ROWS, 0:32] + share.reshape(8, 32, C)
        state[OWN_ROWS, 0:32] = after
        low = after.astype(BF16)
        edge_ns[1] = low
        edge_ew[1, 0] = after[:, 0:8].astype(BF16)
        edge_ew[1, 1] = after[:, 24:32].astype(BF16)
        for step in range(1, tile_size):
            tile_copy(0, step, partial_send.at[0], partial_recv.at[step]).wait_send()
            tile_copy(1, step, summed_all.at[t], summed_all.at[t]).wait_send()
            tile_copy(2, step, attention_all.at[t], attention_all.at[t]).wait_send()
        for step in range(1, ctx_size):
            ctx_copy(step, keys_values.at[g], keys_values.at[g]).wait_send()

    def half_window(half, _):
        @pl.when(half == 0)
        def _():
            for copy in edge_copies:
                copy.wait()
            exchange(0, True)
            extra_low[...] = extra[...].astype(BF16)
            weight_copies[0].wait()
            weight_copies[1].wait()
            drain(0, True)

        @pl.when(half == 1)
        def _():
            context()
            exchange(1, False)
            drain(1, False)

        for r in range(HALF):
            advance(half, r)
        return 0

    lax.fori_loop(0, 2, half_window, 0)
    state_out[...] = state[OWN_ROWS, 0:32].astype(BF16)


def local(
    syndrome_bits,
    region_assign,
    state_in,
    bit_to_candidate,
    bit_to_gate,
    conv_weight,
    gate_weight,
    gate_bias,
    pool_weight,
    region_embed,
    attn_norm_gain,
    query_weight,
    key_weight,
    value_weight,
    out_weight,
    mlp_norm_gain,
    mlp_up,
    mlp_down,
    return_weight,
):
    rows, cols = state_in.shape[0], state_in.shape[1]
    bits = syndrome_bits.transpose(2, 3, 0, 1).reshape(rows, cols, 2 * ROUNDS)
    assign = jnp.broadcast_to(
        region_assign[:, None, :, None], (rows // 2, 2, cols // 2, 2)
    ).reshape(rows, cols, 1)
    ones = jnp.ones((rows, cols, 2), jnp.int32)
    extra = jnp.concatenate(
        [
            bits,
            bits,
            ones,
            jnp.zeros((rows, cols, ASSIGN - 34), jnp.int32),
            assign,
            jnp.zeros((rows, cols, LANES - ASSIGN - 1), jnp.int32),
        ],
        axis=-1,
    ).astype(BF16)
    vmem = pl.BlockSpec(memory_space=pltpu.VMEM)
    hbm = pl.BlockSpec(memory_space=pl.ANY)
    dma = pltpu.SemaphoreType.DMA
    return pl.pallas_call(
        window,
        out_shape=(
            jax.ShapeDtypeStruct((rows, cols, C), BF16),
            jax.ShapeDtypeStruct((128, E), BF16),
        ),
        in_specs=[
            hbm, hbm, vmem, vmem, hbm, hbm, vmem, hbm, hbm, vmem,
            hbm, hbm, hbm, hbm, vmem, hbm, hbm, hbm,
        ],
        out_specs=(vmem, vmem),
        scratch_shapes=[
            pltpu.VMEM((ROWS, COLS, C), F32),
            pltpu.VMEM((ROWS, COLS, 3 * C), BF16),
            pltpu.VMEM((ROWS, COLS, LANES), F32),
            pltpu.VMEM((ROWS, COLS, LANES), BF16),
            pltpu.VMEM((LANES, 2 * C), F32),
            pltpu.VMEM((9, C, C), BF16),
            pltpu.VMEM((C, C), BF16),
            pltpu.VMEM((C, E), BF16),
            pltpu.VMEM((128, E), BF16),
            pltpu.VMEM((3, E, HDIM), BF16),
            pltpu.VMEM((E, E), BF16),
            pltpu.VMEM((E, 2 * E), BF16),
            pltpu.VMEM((2 * E, E), BF16),
            pltpu.VMEM((E, C), BF16),
            pltpu.VMEM((2, 8, 32, C), BF16),
            pltpu.VMEM((2, 2, 8, 8, C), BF16),
            pltpu.VMEM((8, 32, LANES), BF16),
            pltpu.VMEM((2, 8, 8, LANES), BF16),
            pltpu.VMEM((2, 2, 4, 32, C), BF16),
            pltpu.VMEM((2, 2, 8, 8, C), BF16),
            pltpu.VMEM((2, 4, 4, 8, C), BF16),
            pltpu.VMEM((2, 4, 32, LANES), BF16),
            pltpu.VMEM((2, 8, 8, LANES), BF16),
            pltpu.VMEM((4, 4, 8, LANES), BF16),
            pltpu.VMEM((16, 8, C), BF16),
            pltpu.VMEM((16, 8, C), BF16),
            pltpu.VMEM((16, 8, C), BF16),
            pltpu.VMEM((128, HDIM), F32),
            pltpu.VMEM((8, 2, 128, HDIM), BF16),
            pltpu.VMEM((16, 64, HDIM), BF16),
            pltpu.VMEM((128, E), BF16),
            dma((11,)),
            dma((6,)),
            dma((3, 8)),
            dma((3, 8)),
            dma((3, 16)),
            dma((3, 16)),
            dma((8,)),
            dma((8,)),
        ],
        compiler_params=pltpu.CompilerParams(
            collective_id=0, has_side_effects=True, vmem_limit_bytes=60 << 20
        ),
        name="window",
    )(
        extra,
        state_in,
        bit_to_candidate,
        bit_to_gate,
        conv_weight,
        gate_weight,
        gate_bias.reshape(1, -1),
        pool_weight,
        region_embed,
        attn_norm_gain.reshape(1, -1),
        query_weight,
        key_weight,
        value_weight,
        out_weight,
        mlp_norm_gain.reshape(1, -1),
        mlp_up,
        mlp_down,
        return_weight,
    )


def solution(mesh):
    return jax.shard_map(
        local,
        mesh=mesh,
        in_specs=(
            P(None, None, "ctx", "tile"),
            P("ctx", "tile"),
            P("ctx", "tile", None),
            P(),
            P(),
            P(),
            P(),
            P(),
            P(),
            P("ctx", None),
            P(),
            P(),
            P(),
            P(),
            P(),
            P(),
            P(),
            P(),
            P(),
        ),
        out_specs=(P("ctx", "tile", None), P("ctx", None)),
        check_vma=False,
    )
```

```python
import functools
import math

import jax
import jax.numpy as jnp
from jax import lax
from jax.experimental import pallas as pl
from jax.experimental.pallas import tpu as pltpu
from jax.sharding import PartitionSpec as P

MESH = pl.DeviceIdType.MESH
BF16 = jnp.bfloat16
F32 = jnp.float32

HEADS = 8
HDIM = 128
ROUNDS = 8
HALF = 4
C = 512
E = 1024
ROWS = 16
COLS = 48
OWN_ROWS = slice(4, 12)
LANES = 128
ASSIGN = 40

WIDE = C + LANES
BLOCKS = COLS // 2

MOVES = ((-1, 0), (1, 0), (0, -1), (0, 1), (-1, -1), (-1, 1), (1, -1), (1, 1))

TILE_STEPS = sorted(
    ((dz, dx, dc) for dz in range(4) for dx in range(2) for dc in range(2) if dz + dx + dc),
    key=lambda s: (-(min(s[0], 4 - s[0]) + s[1]), s),
)
CTX_STEPS = sorted(
    ((dx, dy) for dx in range(2) for dy in range(4) if dx + dy),
    key=lambda s: (-(2 * s[0] + min(s[1], 4 - s[1])), s),
)


def dot(left, right):
    return jnp.dot(left, right, preferred_element_type=F32)


def rms_norm(values, gain):
    return values * lax.rsqrt(jnp.mean(values * values, axis=-1, keepdims=True) + 1e-05) * gain


def window(
    syndrome_bits,
    region_assign,
    state_in,
    bit_to_candidate,
    bit_to_gate,
    conv_weight,
    gate_weight,
    gate_bias,
    pool_weight,
    region_embed,
    attn_norm_gain,
    query_weight,
    key_weight,
    value_weight,
    out_weight,
    mlp_norm_gain,
    mlp_up,
    mlp_down,
    return_weight,
    state_out,
    context_out,
    bits,
    assign_in,
    to_candidate,
    to_gate,
    bias_in,
    attn_gain,
    mlp_gain,
    state,
    taps,
    extra,
    extra_low,
    drive,
    conv_w,
    gate_w,
    pool_w,
    embed_w,
    qkv_w,
    out_w,
    up_w,
    down_w,
    return_w,
    first_ns,
    first_ew,
    first_halo_ns,
    first_halo_ew,
    first_halo_corner,
    edge_ns,
    edge_ew,
    halo_ns,
    halo_ew,
    halo_corner,
    partial_send,
    partial_recv,
    summed_all,
    queries,
    keys_values,
    attention_all,
    attention_full,
    member_cells,
    member_blocks,
    share_send,
    share_recv,
    small_sem,
    weight_sem,
    edge_sem,
    halo_send,
    halo_recv,
    tile_send,
    tile_recv,
    ctx_send,
    ctx_recv,
    relay_send,
    relay_recv,
    share_sems,
):
    g, t = lax.axis_index("ctx"), lax.axis_index("tile")
    ctx_size, tile_size = 8, 16
    head, part = t // 2, lax.rem(t, 2)

    def tile_peer(step, sign):
        dz, dx, dc = step
        z = lax.rem(t // 4 + (dz if sign > 0 else 4 - dz), 4)
        x = lax.rem(lax.rem(t // 2, 2) + dx, 2)
        core = lax.rem(t + dc, 2)
        return z * 4 + x * 2 + core

    def ctx_peer(step, sign):
        dx, dy = step
        x = lax.rem(g // 4 + dx, 2)
        y = lax.rem(g + (dy if sign > 0 else 4 - dy), 4)
        return x * 4 + y

    def inside(move, sign):
        dg, dt = move
        peer_g, peer_t = g + sign * dg, t + sign * dt
        return (peer_g >= 0) & (peer_g < ctx_size) & (peer_t >= 0) & (peer_t < tile_size)

    barrier = pltpu.get_barrier_semaphore()
    heard = jnp.int32(0)
    for move in MOVES[4:]:
        @pl.when(inside(move, 1))
        def _(move=move):
            pl.semaphore_signal(
                barrier, 1, device_id=(g + move[0], t + move[1]), device_id_type=MESH
            )
        heard += inside(move, -1).astype(jnp.int32)
    for step in CTX_STEPS:
        pl.semaphore_signal(barrier, 1, device_id=(ctx_peer(step, 1), t), device_id_type=MESH)
    for step in TILE_STEPS:
        pl.semaphore_signal(barrier, 1, device_id=(g, tile_peer(step, 1)), device_id_type=MESH)

    small_copies = [
        pltpu.make_async_copy(src, dst, small_sem.at[i])
        for i, (src, dst) in enumerate(
            (
                (syndrome_bits, bits),
                (region_assign, assign_in),
                (bit_to_candidate, to_candidate),
                (bit_to_gate, to_gate),
                (gate_bias, bias_in),
                (attn_norm_gain, attn_gain),
                (mlp_norm_gain, mlp_gain),
            )
        )
    ]
    edge_copies = [
        pltpu.make_async_copy(state_in, first_ns.at[:, :, 0:C], edge_sem.at[0]),
        pltpu.make_async_copy(state_in.at[:, 0:8], first_ew.at[0, :, :, 0:C], edge_sem.at[1]),
        pltpu.make_async_copy(state_in.at[:, 24:32], first_ew.at[1, :, :, 0:C], edge_sem.at[2]),
    ]
    head_cols = pl.ds(pl.multiple_of(head * HDIM, HDIM), HDIM)
    weight_copies = [
        pltpu.make_async_copy(src, dst, weight_sem.at[i])
        for i, (src, dst) in enumerate(
            (
                (conv_weight, conv_w),
                (gate_weight, gate_w),
                (pool_weight, pool_w),
                (region_embed, embed_w),
                (query_weight.at[:, head_cols], qkv_w.at[0]),
                (key_weight.at[:, head_cols], qkv_w.at[1]),
                (value_weight.at[:, head_cols], qkv_w.at[2]),
                (out_weight, out_w),
                (mlp_up, up_w),
                (mlp_down, down_w),
                (return_weight, return_w),
            )
        )
    ]
    for copy in small_copies + edge_copies + weight_copies:
        copy.start()

    state[...] = jnp.zeros_like(state)
    extra[...] = jnp.zeros_like(extra)
    for copy in small_copies:
        copy.wait()

    flat = bits[...].reshape(2 * ROUNDS * 8, 32).astype(F32).astype(BF16)
    source = lax.broadcasted_iota(jnp.int32, (128, 8 * LANES), 0)
    place_to = lax.broadcasted_iota(jnp.int32, (128, 8 * LANES), 1)
    target_row, target_lane = place_to // LANES, lax.rem(place_to, LANES)
    spread = (
        (lax.rem(source, 8) == target_row)
        & (target_lane < 32)
        & (lax.rem(target_lane, 16) == source // 8)
    )
    by_row = lax.dot_general(
        flat,
        spread.astype(F32).astype(BF16),
        (((0,), (0,)), ((), ())),
        preferred_element_type=F32,
    )
    block_of = (
        lax.broadcasted_iota(jnp.int32, (32, 16), 0) // 2
        == lax.broadcasted_iota(jnp.int32, (32, 16), 1)
    )
    assign_lane = (
        (lax.broadcasted_iota(jnp.int32, (16, LANES), 1) == ASSIGN).astype(F32).astype(BF16)
    )
    lane = lax.broadcasted_iota(jnp.int32, (32, LANES), 1)
    ones = ((lane == 32) | (lane == 33)).astype(F32)
    for i in range(8):
        tokens_of = jnp.where(
            block_of, assign_in[i // 2 : i // 2 + 1].astype(F32), 0.0
        ).astype(BF16)
        row = by_row[:, i * LANES : (i + 1) * LANES] + dot(tokens_of, assign_lane) + ones
        extra[4 + i, 0:32] = row
        first_ns[i, :, C:WIDE] = row.astype(BF16)
        first_ew[0, i, :, C:WIDE] = row[0:8].astype(BF16)
        first_ew[1, i, :, C:WIDE] = row[24:32].astype(BF16)

    lane_row = lax.broadcasted_iota(jnp.int32, (LANES, 2 * C), 0)
    both = jnp.concatenate([to_candidate[...], to_gate[...]], axis=1)
    bias = jnp.concatenate([jnp.zeros_like(bias_in[...]), bias_in[...]], axis=1)
    both_high = both.astype(BF16).astype(F32)
    both_low = both - both_high
    bias_high = bias.astype(BF16).astype(F32)
    bias_low = bias - bias_high
    even_row = lax.rem(lane_row, 2) == 0
    drive[...] = jnp.where(
        lane_row < 16,
        jnp.where(even_row, both_high[0:1], both_high[1:2]),
        jnp.where(
            lane_row < 32,
            jnp.where(even_row, both_low[0:1], both_low[1:2]),
            jnp.where(
                lane_row == 32, bias_high, jnp.where(lane_row == 33, bias_low, 0.0)
            ),
        ),
    )

    column = lax.broadcasted_iota(jnp.int32, (COLS, 1), 0)
    column_inside = ~(
        ((t == 0) & (column >= 40))
        | ((t == tile_size - 1) & (column >= 32) & (column < 40))
    )

    def halo_parts(move, half):
        dg, dt = move
        index = MOVES.index(move)
        rows = {0: slice(0, 8), -1: slice(0, 4), 1: slice(4, 8)}[dg]
        side = 0 if dt == -1 else 1
        ns, ew = (edge_ns, edge_ew) if half else (first_ns, first_ew)
        if dt == 0:
            return ns.at[rows], (halo_ns if half else first_halo_ns).at[index]
        if dg == 0:
            return ew.at[side], (halo_ew if half else first_halo_ew).at[side]
        return ew.at[side, rows], (halo_corner if half else first_halo_corner).at[index - 4]

    def halo_copy(move, half):
        source, target = halo_parts(move, half)
        index = MOVES.index(move)
        return pltpu.make_async_remote_copy(
            src_ref=source,
            dst_ref=target,
            send_sem=halo_send.at[half, index],
            recv_sem=halo_recv.at[half, index],
            device_id=(g + move[0], t + move[1]),
            device_id_type=MESH,
        )

    def send_halos(half):
        for move in MOVES:
            @pl.when(inside(move, 1))
            def _(move=move):
                halo_copy(move, half).start()

    def drain_halos(half):
        for move in MOVES:
            @pl.when(inside(move, 1))
            def _(move=move):
                halo_copy(move, half).wait_send()

    def take_halos(moves, half):
        for move in moves:
            @pl.when(inside(move, -1))
            def _(move=move):
                dg, dt = move
                rows = {0: slice(4, 12), -1: slice(12, 16), 1: slice(0, 4)}[dg]
                cols = {0: slice(0, 32), -1: slice(32, 40), 1: slice(40, 48)}[dt]
                halo_copy(move, half).wait_recv()
                _, target = halo_parts(move, half)
                if half:
                    state[rows, cols] = target[...].astype(F32)
                else:
                    state[rows, cols] = target[:, :, 0:C].astype(F32)
                    extra[rows, cols] = target[:, :, C:WIDE].astype(F32)

    beside, beyond = MOVES[2:4], MOVES[0:2] + MOVES[4:8]

    def fill_taps(level, rows):
        for i in rows:
            row = state[i]
            taps[level, i, :, 0:C] = pltpu.roll(row, 1, 0).astype(BF16)
            taps[level, i, :, C : 2 * C] = row.astype(BF16)
            taps[level, i, :, 2 * C : 3 * C] = pltpu.roll(row, COLS - 1, 0).astype(BF16)

    def advance(half, level, spans, width):
        round_index = half * HALF + level
        lane = lax.broadcasted_iota(jnp.int32, (LANES, 2 * C), 0)
        chosen = ((lane < 32) & (lax.rem(lane, 16) // 2 == round_index)) | (lane >= 32)
        drive_now = jnp.where(chosen, drive[...], 0.0).astype(BF16)
        count = sum(high - low for low, high in spans) * width

        def cells(read):
            parts = [read(low, high) for low, high in spans]
            whole = parts[0] if len(parts) == 1 else jnp.concatenate(parts, axis=0)
            return whole.reshape(count, whole.shape[-1])

        flags = cells(lambda low, high: extra_low[low:high, 0:width])
        candidate = dot(flags, drive_now[:, 0:C])
        for a in range(3):
            candidate += dot(
                cells(lambda low, high: taps[level, low + a - 1 : high + a - 1, 0:width]),
                conv_w[3 * a : 3 * a + 3].reshape(3 * C, C),
            )
        gate = dot(
            cells(lambda low, high: taps[level, low:high, 0:width, C : 2 * C]), gate_w[...]
        ) + dot(flags, drive_now[:, C : 2 * C])
        update = 0.5 + 0.5 * jnp.tanh(0.5 * gate)
        before = cells(lambda low, high: state[low:high, 0:width])
        after = before + update * (jnp.tanh(candidate) - before)
        after = after.reshape(count // width, width, C)
        at = 0
        for low, high in spans:
            for i in range(low, high):
                if width < COLS:
                    state[i, 0:width] = after[at]
                else:
                    keep = column_inside
                    if i < 4:
                        keep = keep & (g > 0)
                    if i >= 12:
                        keep = keep & (g < ctx_size - 1)
                    state[i] = jnp.where(keep, after[at], 0.0)
                at += 1

    def tile_copy(phase, index, source, target):
        return pltpu.make_async_remote_copy(
            src_ref=source,
            dst_ref=target,
            send_sem=tile_send.at[phase, index],
            recv_sem=tile_recv.at[phase, index],
            device_id=(g, tile_peer(TILE_STEPS[index], 1)),
            device_id_type=MESH,
        )

    mine = pl.ds(pl.multiple_of(part * 64, 64), 64)

    def ctx_copy(index, owner):
        block = keys_values.at[owner, :, mine]
        return pltpu.make_async_remote_copy(
            src_ref=block,
            dst_ref=block,
            send_sem=ctx_send.at[index],
            recv_sem=ctx_recv.at[index],
            device_id=(ctx_peer(CTX_STEPS[index], 1), t),
            device_id_type=MESH,
        )

    def relay_copy(index, owner, which):
        block = keys_values.at[owner, :, which]
        return pltpu.make_async_remote_copy(
            src_ref=block,
            dst_ref=block,
            send_sem=relay_send.at[index],
            recv_sem=relay_recv.at[index],
            device_id=(g, t + 1 - 2 * part),
            device_id_type=MESH,
        )

    def share_copy(index):
        return pltpu.make_async_remote_copy(
            src_ref=share_send.at[index],
            dst_ref=share_recv.at[index],
            send_sem=share_sems.at[0, index],
            recv_sem=share_sems.at[1, index],
            device_id=(g + MOVES[index][0], t),
            device_id_type=MESH,
        )

    tile_steps, ctx_steps = range(len(TILE_STEPS)), range(len(CTX_STEPS))
    token_lane = lax.broadcasted_iota(jnp.int32, (128, 128), 1).astype(F32)

    def one_hot(tokens):
        count = tokens.shape[0]
        lanes = lax.broadcasted_iota(jnp.int32, (count, 128), 1).astype(F32)
        return (tokens == lanes).astype(F32).astype(BF16)

    def context():
        pooled = []
        for i in range(4, 12, 2):
            pair = state[i, 0:32] + state[i + 1, 0:32]
            pooled.append(((pair + pltpu.roll(pair, 31, 0)) * 0.25).astype(BF16))
        pooled = jnp.concatenate(pooled, axis=0)
        assign = jnp.concatenate(
            [extra[i, 0:32, ASSIGN : ASSIGN + 1] for i in range(4, 12, 2)], axis=0
        )
        even = lax.rem(lax.broadcasted_iota(jnp.int32, (128, 128), 0), 2) == 0
        member = ((assign == token_lane) & even).astype(F32).astype(BF16)
        partial = lax.dot_general(
            member, pooled, (((0,), (0,)), ((), ())), preferred_element_type=F32
        )
        partial_send[...] = partial.reshape(tile_size, 8, C).astype(BF16)
        for k in tile_steps:
            tile_copy(
                0, k, partial_send.at[tile_peer(TILE_STEPS[k], 1)], partial_recv.at[k]
            ).start()
        own = state[OWN_ROWS, 0:32]
        edge_ns[...] = own.astype(BF16)
        edge_ew[0] = own[:, 0:8].astype(BF16)
        edge_ew[1] = own[:, 24:32].astype(BF16)
        member_cells[...] = one_hot(
            extra[OWN_ROWS, :, ASSIGN : ASSIGN + 1].reshape(8 * COLS, 1)
        )
        pick = (
            (
                lax.broadcasted_iota(jnp.int32, (BLOCKS, COLS), 0) * 2
                == lax.broadcasted_iota(jnp.int32, (BLOCKS, COLS), 1)
            )
            .astype(F32)
            .astype(BF16)
        )
        for side in range(2):
            for k in range(2):
                tokens_of = dot(pick, extra_low[4 + 4 * side + 2 * k])[:, ASSIGN : ASSIGN + 1]
                member_blocks[side, k * BLOCKS : (k + 1) * BLOCKS] = one_hot(tokens_of)
        total = partial_send[t].astype(F32)
        for k in tile_steps:
            tile_copy(0, k, partial_send.at[0], partial_recv.at[k]).wait_recv()
            total += partial_recv[k].astype(F32)
        summed_all[t] = total.astype(BF16)
        for k in tile_steps:
            tile_copy(1, k, summed_all.at[t], summed_all.at[t]).start()
        for copy in weight_copies[2:7]:
            copy.wait()
        for k in tile_steps:
            sender = tile_peer(TILE_STEPS[k], -1)
            tile_copy(1, k, summed_all.at[t], summed_all.at[sender]).wait_recv()
        summed = summed_all[...].reshape(128, C)
        tokens = embed_w[...].astype(F32) + dot(summed, pool_w[...])
        normed = rms_norm(tokens, attn_gain[...]).astype(BF16)
        keys_values[g, 0] = dot(normed, qkv_w[1]).astype(BF16)
        keys_values[g, 1] = dot(normed, qkv_w[2]).astype(BF16)
        for k in ctx_steps:
            ctx_copy(k, g).start()
        queries[...] = dot(normed, qkv_w[0])
        other = pl.ds(pl.multiple_of((1 - part) * 64, 64), 64)
        for k in reversed(ctx_steps):
            sender = ctx_peer(CTX_STEPS[k], -1)
            ctx_copy(k, sender).wait_recv()
            relay_copy(k, sender, mine).start()
        for k in reversed(ctx_steps):
            relay_copy(k, ctx_peer(CTX_STEPS[k], -1), other).wait_recv()
        send_halos(1)
        query = queries[mine].astype(BF16)
        scores = jnp.concatenate(
            [
                lax.dot_general(
                    query,
                    keys_values[i, 0],
                    (((1,), (1,)), ((), ())),
                    preferred_element_type=F32,
                )
                for i in range(ctx_size)
            ],
            axis=1,
        ) * (1.0 / math.sqrt(HDIM))
        weights = jnp.exp(scores - jnp.max(scores, axis=-1, keepdims=True))
        denominator = jnp.sum(weights, axis=-1, keepdims=True)
        weights_low = weights.astype(BF16)
        weighted = dot(
            weights_low, jnp.concatenate([keys_values[i, 1] for i in range(ctx_size)], axis=0)
        )
        attention_all[t] = (weighted / denominator).astype(BF16)
        for k in tile_steps:
            tile_copy(2, k, attention_all.at[t], attention_all.at[t]).start()
        for copy in weight_copies[7:]:
            copy.wait()
        for k in tile_steps:
            sender = tile_peer(TILE_STEPS[k], -1)
            tile_copy(2, k, attention_all.at[t], attention_all.at[sender]).wait_recv()
        for i in range(tile_size):
            attention_full[
                (i % 2) * 64 : (i % 2) * 64 + 64, (i // 2) * HDIM : (i // 2 + 1) * HDIM
            ] = attention_all[i]
        attended = tokens + dot(attention_full[...], out_w[...])
        mlp_in = rms_norm(attended, mlp_gain[...]).astype(BF16)
        hidden = jax.nn.gelu(dot(mlp_in, up_w[...])).astype(BF16)
        context = (attended + dot(hidden, down_w[...])).astype(BF16)
        returned = dot(context, return_w[...])
        returned_high = returned.astype(BF16)
        for side in range(2):
            share_send[side] = (
                dot(member_blocks[side], returned_high).reshape(2, BLOCKS, C).astype(BF16)
            )
            @pl.when(inside(MOVES[side], 1))
            def _(side=side):
                share_copy(side).start()
        context_out[...] = context
        returned_low = (returned - returned_high.astype(F32)).astype(BF16)
        take_halos(beside, 1)
        share = dot(member_cells[...], returned_high) + dot(member_cells[...], returned_low)
        share = share.reshape(8, COLS, C)
        for i in range(8):
            state[4 + i] += jnp.where(column_inside, share[i], 0.0)

    def take_shares():
        take_halos(beyond, 1)
        unpick = (
            (
                lax.broadcasted_iota(jnp.int32, (COLS, BLOCKS), 0) // 2
                == lax.broadcasted_iota(jnp.int32, (COLS, BLOCKS), 1)
            )
            .astype(F32)
            .astype(BF16)
        )
        for side in range(2):
            @pl.when(inside(MOVES[side], -1))
            def _(side=side):
                share_copy(side).wait_recv()
                first = 12 if side == 0 else 0
                for k in range(2):
                    share = jnp.where(column_inside, dot(unpick, share_recv[side, k]), 0.0)
                    state[first + 2 * k] += share
                    state[first + 2 * k + 1] += share

    def half_window(half, _):
        @pl.when(half == 0)
        def _():
            for copy in edge_copies:
                copy.wait()
            pl.semaphore_wait(barrier, heard + (ctx_size - 1) + (tile_size - 1))
            send_halos(0)
            state[OWN_ROWS, 0:32] = first_ns[:, :, 0:C].astype(F32)
            take_halos(beside, 0)
            extra_low[OWN_ROWS] = extra[OWN_ROWS].astype(BF16)
            weight_copies[0].wait()
            weight_copies[1].wait()

        @pl.when(half == 1)
        def _():
            context()

        for level in range(HALF):
            fill_taps(level, range(4 + level, 12 - level))
            if level < HALF - 1:
                advance(half, level, ((5 + level, 11 - level),), COLS)

        @pl.when(half == 0)
        def _():
            take_halos(beyond, 0)
            extra_low[0:4] = extra[0:4].astype(BF16)
            extra_low[12:16] = extra[12:16].astype(BF16)

        @pl.when(half == 1)
        def _():
            take_shares()

        for level in range(HALF):
            fill_taps(level, (*range(level, 4 + level), *range(12 - level, 16 - level)))
            if level < HALF - 1:
                spans = ((1 + level, 5 + level), (11 - level, 15 - level))
                advance(half, level, spans, COLS)
            else:
                advance(half, level, ((4, 12),), 32)
        return 0

    lax.fori_loop(0, 2, half_window, 0)
    state_out[...] = state[OWN_ROWS, 0:32].astype(BF16)
    drain_halos(0)
    drain_halos(1)
    for k in tile_steps:
        tile_copy(0, k, partial_send.at[0], partial_recv.at[k]).wait_send()
        tile_copy(1, k, summed_all.at[t], summed_all.at[t]).wait_send()
        tile_copy(2, k, attention_all.at[t], attention_all.at[t]).wait_send()
    for k in ctx_steps:
        ctx_copy(k, g).wait_send()
        relay_copy(k, g, mine).wait_send()
    for side in range(2):
        @pl.when(inside(MOVES[side], 1))
        def _(side=side):
            share_copy(side).wait_send()


def local(
    syndrome_bits,
    region_assign,
    state_in,
    bit_to_candidate,
    bit_to_gate,
    conv_weight,
    gate_weight,
    gate_bias,
    pool_weight,
    region_embed,
    attn_norm_gain,
    query_weight,
    key_weight,
    value_weight,
    out_weight,
    mlp_norm_gain,
    mlp_up,
    mlp_down,
    return_weight,
):
    rows, cols = state_in.shape[0], state_in.shape[1]
    hbm = pl.BlockSpec(memory_space=pl.ANY)
    vmem = pl.BlockSpec(memory_space=pltpu.VMEM)
    dma = pltpu.SemaphoreType.DMA
    return pl.pallas_call(
        window,
        out_shape=(
            pltpu.VMEM((rows, cols, C), BF16),
            pltpu.VMEM((128, E), BF16),
        ),
        in_specs=[hbm] * 19,
        out_specs=(vmem, vmem),
        scratch_shapes=[
            pltpu.VMEM((ROUNDS, 2, 8, 32), jnp.int32),
            pltpu.VMEM((4, 16), jnp.int32),
            pltpu.VMEM((2, C), F32),
            pltpu.VMEM((2, C), F32),
            pltpu.VMEM((1, C), F32),
            pltpu.VMEM((1, E), F32),
            pltpu.VMEM((1, E), F32),
            pltpu.VMEM((ROWS, COLS, C), F32),
            pltpu.VMEM((HALF, ROWS, COLS, 3 * C), BF16),
            pltpu.VMEM((ROWS, COLS, LANES), F32),
            pltpu.VMEM((ROWS, COLS, LANES), BF16),
            pltpu.VMEM((LANES, 2 * C), F32),
            pltpu.VMEM((9, C, C), BF16),
            pltpu.VMEM((C, C), BF16),
            pltpu.VMEM((C, E), BF16),
            pltpu.VMEM((128, E), BF16),
            pltpu.VMEM((3, E, HDIM), BF16),
            pltpu.VMEM((E, E), BF16),
            pltpu.VMEM((E, 2 * E), BF16),
            pltpu.VMEM((2 * E, E), BF16),
            pltpu.VMEM((E, C), BF16),
            pltpu.VMEM((8, 32, WIDE), BF16),
            pltpu.VMEM((2, 8, 8, WIDE), BF16),
            pltpu.VMEM((2, 4, 32, WIDE), BF16),
            pltpu.VMEM((2, 8, 8, WIDE), BF16),
            pltpu.VMEM((4, 4, 8, WIDE), BF16),
            pltpu.VMEM((8, 32, C), BF16),
            pltpu.VMEM((2, 8, 8, C), BF16),
            pltpu.VMEM((2, 4, 32, C), BF16),
            pltpu.VMEM((2, 8, 8, C), BF16),
            pltpu.VMEM((4, 4, 8, C), BF16),
            pltpu.VMEM((16, 8, C), BF16),
            pltpu.VMEM((15, 8, C), BF16),
            pltpu.VMEM((16, 8, C), BF16),
            pltpu.VMEM((128, HDIM), F32),
            pltpu.VMEM((8, 2, 128, HDIM), BF16),
            pltpu.VMEM((16, 64, HDIM), BF16),
            pltpu.VMEM((128, E), BF16),
            pltpu.VMEM((8 * COLS, 128), BF16),
            pltpu.VMEM((2, 2 * BLOCKS, 128), BF16),
            pltpu.VMEM((2, 2, BLOCKS, C), BF16),
            pltpu.VMEM((2, 2, BLOCKS, C), BF16),
            dma((7,)),
            dma((11,)),
            dma((3,)),
            dma((2, 8)),
            dma((2, 8)),
            dma((3, 15)),
            dma((3, 15)),
            dma((7,)),
            dma((7,)),
            dma((7,)),
            dma((7,)),
            dma((2, 2)),
        ],
        compiler_params=pltpu.CompilerParams(
            collective_id=0, has_side_effects=True, vmem_limit_bytes=62 << 20
        ),
        name="window",
    )(
        syndrome_bits,
        region_assign,
        state_in,
        bit_to_candidate,
        bit_to_gate,
        conv_weight,
        gate_weight,
        gate_bias.reshape(1, -1),
        pool_weight,
        region_embed,
        attn_norm_gain.reshape(1, -1),
        query_weight,
        key_weight,
        value_weight,
        out_weight,
        mlp_norm_gain.reshape(1, -1),
        mlp_up,
        mlp_down,
        return_weight,
    )


def solution(mesh):
    return jax.shard_map(
        local,
        mesh=mesh,
        in_specs=(
            P(None, None, "ctx", "tile"),
            P("ctx", "tile"),
            P("ctx", "tile", None),
            P(),
            P(),
            P(),
            P(),
            P(),
            P(),
            P("ctx", None),
            P(),
            P(),
            P(),
            P(),
            P(),
            P(),
            P(),
            P(),
            P(),
        ),
        out_specs=(P("ctx", "tile", None), P("ctx", None)),
        check_vma=False,
    )
```

```python
import functools
import math

import jax
import jax.numpy as jnp
from jax import lax
from jax.experimental import pallas as pl
from jax.experimental.pallas import tpu as pltpu
from jax.sharding import PartitionSpec as P

MESH = pl.DeviceIdType.MESH
BF16 = jnp.bfloat16
F32 = jnp.float32

HEADS = 8
HDIM = 128
ROUNDS = 8
HALF = 4
C = 512
E = 1024
ROWS = 16
COLS = 48
OWN_ROWS = slice(4, 12)
LANES = 128
ASSIGN = 40

WIDE = C + LANES
BLOCKS = COLS // 2

MOVES = ((-1, 0), (1, 0), (0, -1), (0, 1), (-1, -1), (-1, 1), (1, -1), (1, 1))

TILE_STEPS = sorted(
    ((dz, dx, dc) for dz in range(4) for dx in range(2) for dc in range(2) if dz + dx + dc),
    key=lambda s: (-(min(s[0], 4 - s[0]) + s[1]), s),
)
CTX_STEPS = sorted(
    ((dx, dy) for dx in range(2) for dy in range(4) if dx + dy),
    key=lambda s: (-(2 * s[0] + min(s[1], 4 - s[1])), s),
)


def dot(left, right):
    return jnp.dot(left, right, preferred_element_type=F32)


def rms_norm(values, gain):
    return values * lax.rsqrt(jnp.mean(values * values, axis=-1, keepdims=True) + 1e-05) * gain


def window(
    syndrome_bits,
    region_assign,
    state_in,
    bit_to_candidate,
    bit_to_gate,
    conv_weight,
    gate_weight,
    gate_bias,
    pool_weight,
    region_embed,
    attn_norm_gain,
    query_weight,
    key_weight,
    value_weight,
    out_weight,
    mlp_norm_gain,
    mlp_up,
    mlp_down,
    return_weight,
    state_out,
    context_out,
    bits,
    assign_in,
    to_candidate,
    to_gate,
    bias_in,
    attn_gain,
    mlp_gain,
    state,
    taps,
    extra,
    extra_low,
    drive,
    conv_w,
    gate_w,
    pool_w,
    embed_w,
    qkv_w,
    out_w,
    up_w,
    down_w,
    return_w,
    first_ns,
    first_ew,
    first_halo_ns,
    first_halo_ew,
    first_halo_corner,
    edge_ns,
    edge_ew,
    halo_ns,
    halo_ew,
    halo_corner,
    partial_send,
    partial_recv,
    summed_all,
    queries,
    keys_values,
    attention_all,
    attention_full,
    member_cells,
    member_blocks,
    share_send,
    share_recv,
    small_sem,
    weight_sem,
    edge_sem,
    halo_send,
    halo_recv,
    tile_send,
    tile_recv,
    ctx_send,
    ctx_recv,
    relay_send,
    relay_recv,
    share_sems,
):
    g, t = lax.axis_index("ctx"), lax.axis_index("tile")
    ctx_size, tile_size = 8, 16
    head, part = t // 2, lax.rem(t, 2)

    def tile_peer(step, sign):
        dz, dx, dc = step
        z = lax.rem(t // 4 + (dz if sign > 0 else 4 - dz), 4)
        x = lax.rem(lax.rem(t // 2, 2) + dx, 2)
        core = lax.rem(t + dc, 2)
        return z * 4 + x * 2 + core

    def ctx_peer(step, sign):
        dx, dy = step
        x = lax.rem(g // 4 + dx, 2)
        y = lax.rem(g + (dy if sign > 0 else 4 - dy), 4)
        return x * 4 + y

    def inside(move, sign):
        dg, dt = move
        peer_g, peer_t = g + sign * dg, t + sign * dt
        return (peer_g >= 0) & (peer_g < ctx_size) & (peer_t >= 0) & (peer_t < tile_size)

    barrier = pltpu.get_barrier_semaphore()
    heard = jnp.int32(0)
    for move in MOVES[4:]:
        @pl.when(inside(move, 1))
        def _(move=move):
            pl.semaphore_signal(
                barrier, 1, device_id=(g + move[0], t + move[1]), device_id_type=MESH
            )
        heard += inside(move, -1).astype(jnp.int32)
    for step in CTX_STEPS:
        pl.semaphore_signal(barrier, 1, device_id=(ctx_peer(step, 1), t), device_id_type=MESH)
    for step in TILE_STEPS:
        pl.semaphore_signal(barrier, 1, device_id=(g, tile_peer(step, 1)), device_id_type=MESH)

    small_copies = [
        pltpu.make_async_copy(src, dst, small_sem.at[i])
        for i, (src, dst) in enumerate(
            (
                (syndrome_bits, bits),
                (region_assign, assign_in),
                (bit_to_candidate, to_candidate),
                (bit_to_gate, to_gate),
                (gate_bias, bias_in),
                (attn_norm_gain, attn_gain),
                (mlp_norm_gain, mlp_gain),
            )
        )
    ]
    edge_copies = [
        pltpu.make_async_copy(state_in, first_ns.at[:, :, 0:C], edge_sem.at[0]),
        pltpu.make_async_copy(state_in.at[:, 0:8], first_ew.at[0, :, :, 0:C], edge_sem.at[1]),
        pltpu.make_async_copy(state_in.at[:, 24:32], first_ew.at[1, :, :, 0:C], edge_sem.at[2]),
    ]
    head_cols = pl.ds(pl.multiple_of(head * HDIM, HDIM), HDIM)
    weight_copies = [
        pltpu.make_async_copy(src, dst, weight_sem.at[i])
        for i, (src, dst) in enumerate(
            (
                (conv_weight, conv_w),
                (gate_weight, gate_w),
                (pool_weight, pool_w),
                (region_embed, embed_w),
                (query_weight.at[:, head_cols], qkv_w.at[0]),
                (key_weight.at[:, head_cols], qkv_w.at[1]),
                (value_weight.at[:, head_cols], qkv_w.at[2]),
                (out_weight, out_w),
                (mlp_up, up_w),
                (mlp_down, down_w),
                (return_weight, return_w),
            )
        )
    ]
    for copy in small_copies + edge_copies + weight_copies[:2]:
        copy.start()

    state[...] = jnp.zeros_like(state)
    extra[...] = jnp.zeros_like(extra)
    for copy in small_copies:
        copy.wait()

    flat = bits[...].reshape(2 * ROUNDS * 8, 32).astype(F32).astype(BF16)
    source = lax.broadcasted_iota(jnp.int32, (128, 8 * LANES), 0)
    place_to = lax.broadcasted_iota(jnp.int32, (128, 8 * LANES), 1)
    target_row, target_lane = place_to // LANES, lax.rem(place_to, LANES)
    spread = (
        (lax.rem(source, 8) == target_row)
        & (target_lane < 32)
        & (lax.rem(target_lane, 16) == source // 8)
    )
    by_row = lax.dot_general(
        flat,
        spread.astype(F32).astype(BF16),
        (((0,), (0,)), ((), ())),
        preferred_element_type=F32,
    )
    block_of = (
        lax.broadcasted_iota(jnp.int32, (32, 16), 0) // 2
        == lax.broadcasted_iota(jnp.int32, (32, 16), 1)
    )
    assign_lane = (
        (lax.broadcasted_iota(jnp.int32, (16, LANES), 1) == ASSIGN).astype(F32).astype(BF16)
    )
    lane = lax.broadcasted_iota(jnp.int32, (32, LANES), 1)
    ones = ((lane == 32) | (lane == 33)).astype(F32)
    for i in range(8):
        tokens_of = jnp.where(
            block_of, assign_in[i // 2 : i // 2 + 1].astype(F32), 0.0
        ).astype(BF16)
        row = by_row[:, i * LANES : (i + 1) * LANES] + dot(tokens_of, assign_lane) + ones
        extra[4 + i, 0:32] = row
        first_ns[i, :, C:WIDE] = row.astype(BF16)
        first_ew[0, i, :, C:WIDE] = row[0:8].astype(BF16)
        first_ew[1, i, :, C:WIDE] = row[24:32].astype(BF16)

    lane_row = lax.broadcasted_iota(jnp.int32, (LANES, 2 * C), 0)
    both = jnp.concatenate([to_candidate[...], to_gate[...]], axis=1)
    bias = jnp.concatenate([jnp.zeros_like(bias_in[...]), bias_in[...]], axis=1)
    both_high = both.astype(BF16).astype(F32)
    both_low = both - both_high
    bias_high = bias.astype(BF16).astype(F32)
    bias_low = bias - bias_high
    even_row = lax.rem(lane_row, 2) == 0
    drive[...] = jnp.where(
        lane_row < 16,
        jnp.where(even_row, both_high[0:1], both_high[1:2]),
        jnp.where(
            lane_row < 32,
            jnp.where(even_row, both_low[0:1], both_low[1:2]),
            jnp.where(
                lane_row == 32, bias_high, jnp.where(lane_row == 33, bias_low, 0.0)
            ),
        ),
    )

    column = lax.broadcasted_iota(jnp.int32, (COLS, 1), 0)
    column_inside = ~(
        ((t == 0) & (column >= 40))
        | ((t == tile_size - 1) & (column >= 32) & (column < 40))
    )

    def halo_parts(move, half):
        dg, dt = move
        index = MOVES.index(move)
        rows = {0: slice(0, 8), -1: slice(0, 4), 1: slice(4, 8)}[dg]
        side = 0 if dt == -1 else 1
        ns, ew = (edge_ns, edge_ew) if half else (first_ns, first_ew)
        if dt == 0:
            return ns.at[rows], (halo_ns if half else first_halo_ns).at[index]
        if dg == 0:
            return ew.at[side], (halo_ew if half else first_halo_ew).at[side]
        return ew.at[side, rows], (halo_corner if half else first_halo_corner).at[index - 4]

    def halo_copy(move, half):
        source, target = halo_parts(move, half)
        index = MOVES.index(move)
        return pltpu.make_async_remote_copy(
            src_ref=source,
            dst_ref=target,
            send_sem=halo_send.at[half, index],
            recv_sem=halo_recv.at[half, index],
            device_id=(g + move[0], t + move[1]),
            device_id_type=MESH,
        )

    def send_halos(half):
        for move in MOVES:
            @pl.when(inside(move, 1))
            def _(move=move):
                halo_copy(move, half).start()

    def drain_halos(half):
        for move in MOVES:
            @pl.when(inside(move, 1))
            def _(move=move):
                halo_copy(move, half).wait_send()

    def take_halos(moves, half):
        for move in moves:
            @pl.when(inside(move, -1))
            def _(move=move):
                dg, dt = move
                rows = {0: slice(4, 12), -1: slice(12, 16), 1: slice(0, 4)}[dg]
                cols = {0: slice(0, 32), -1: slice(32, 40), 1: slice(40, 48)}[dt]
                halo_copy(move, half).wait_recv()
                _, target = halo_parts(move, half)
                if half:
                    state[rows, cols] = target[...].astype(F32)
                else:
                    state[rows, cols] = target[:, :, 0:C].astype(F32)
                    extra[rows, cols] = target[:, :, C:WIDE].astype(F32)

    beside, beyond = MOVES[2:4], MOVES[0:2] + MOVES[4:8]

    def fill_taps(level, rows):
        for i in rows:
            row = state[i]
            taps[level, i, :, 0:C] = pltpu.roll(row, 1, 0).astype(BF16)
            taps[level, i, :, C : 2 * C] = row.astype(BF16)
            taps[level, i, :, 2 * C : 3 * C] = pltpu.roll(row, COLS - 1, 0).astype(BF16)

    def advance(half, level, spans, width):
        round_index = half * HALF + level
        lane = lax.broadcasted_iota(jnp.int32, (LANES, 2 * C), 0)
        chosen = ((lane < 32) & (lax.rem(lane, 16) // 2 == round_index)) | (lane >= 32)
        drive_now = jnp.where(chosen, drive[...], 0.0).astype(BF16)
        count = sum(high - low for low, high in spans) * width

        def cells(read):
            parts = [read(low, high) for low, high in spans]
            whole = parts[0] if len(parts) == 1 else jnp.concatenate(parts, axis=0)
            return whole.reshape(count, whole.shape[-1])

        flags = cells(lambda low, high: extra_low[low:high, 0:width])
        candidate = dot(flags, drive_now[:, 0:C])
        for a in range(3):
            candidate += dot(
                cells(lambda low, high: taps[level, low + a - 1 : high + a - 1, 0:width]),
                conv_w[3 * a : 3 * a + 3].reshape(3 * C, C),
            )
        gate = dot(
            cells(lambda low, high: taps[level, low:high, 0:width, C : 2 * C]), gate_w[...]
        ) + dot(flags, drive_now[:, C : 2 * C])
        update = 0.5 + 0.5 * jnp.tanh(0.5 * gate)
        before = cells(lambda low, high: state[low:high, 0:width])
        after = before + update * (jnp.tanh(candidate) - before)
        after = after.reshape(count // width, width, C)
        at = 0
        for low, high in spans:
            for i in range(low, high):
                if width < COLS:
                    state[i, 0:width] = after[at]
                else:
                    keep = column_inside
                    if i < 4:
                        keep = keep & (g > 0)
                    if i >= 12:
                        keep = keep & (g < ctx_size - 1)
                    state[i] = jnp.where(keep, after[at], 0.0)
                at += 1

    def tile_copy(phase, index, source, target):
        return pltpu.make_async_remote_copy(
            src_ref=source,
            dst_ref=target,
            send_sem=tile_send.at[phase, index],
            recv_sem=tile_recv.at[phase, index],
            device_id=(g, tile_peer(TILE_STEPS[index], 1)),
            device_id_type=MESH,
        )

    mine = pl.ds(pl.multiple_of(part * 64, 64), 64)

    def ctx_copy(index, owner):
        block = keys_values.at[owner, :, mine]
        return pltpu.make_async_remote_copy(
            src_ref=block,
            dst_ref=block,
            send_sem=ctx_send.at[index],
            recv_sem=ctx_recv.at[index],
            device_id=(ctx_peer(CTX_STEPS[index], 1), t),
            device_id_type=MESH,
        )

    def relay_copy(index, owner, which):
        block = keys_values.at[owner, :, which]
        return pltpu.make_async_remote_copy(
            src_ref=block,
            dst_ref=block,
            send_sem=relay_send.at[index],
            recv_sem=relay_recv.at[index],
            device_id=(g, t + 1 - 2 * part),
            device_id_type=MESH,
        )

    def share_copy(index):
        return pltpu.make_async_remote_copy(
            src_ref=share_send.at[index],
            dst_ref=share_recv.at[index],
            send_sem=share_sems.at[0, index],
            recv_sem=share_sems.at[1, index],
            device_id=(g + MOVES[index][0], t),
            device_id_type=MESH,
        )

    tile_steps, ctx_steps = range(len(TILE_STEPS)), range(len(CTX_STEPS))
    token_lane = lax.broadcasted_iota(jnp.int32, (128, 128), 1).astype(F32)

    def one_hot(tokens):
        count = tokens.shape[0]
        lanes = lax.broadcasted_iota(jnp.int32, (count, 128), 1).astype(F32)
        return (tokens == lanes).astype(F32).astype(BF16)

    def context():
        pooled = []
        for i in range(4, 12, 2):
            pair = state[i, 0:32] + state[i + 1, 0:32]
            pooled.append(((pair + pltpu.roll(pair, 31, 0)) * 0.25).astype(BF16))
        pooled = jnp.concatenate(pooled, axis=0)
        assign = jnp.concatenate(
            [extra[i, 0:32, ASSIGN : ASSIGN + 1] for i in range(4, 12, 2)], axis=0
        )
        even = lax.rem(lax.broadcasted_iota(jnp.int32, (128, 128), 0), 2) == 0
        member = ((assign == token_lane) & even).astype(F32).astype(BF16)
        partial = lax.dot_general(
            member, pooled, (((0,), (0,)), ((), ())), preferred_element_type=F32
        )
        partial_send[...] = partial.reshape(tile_size, 8, C).astype(BF16)
        for k in tile_steps:
            tile_copy(
                0, k, partial_send.at[tile_peer(TILE_STEPS[k], 1)], partial_recv.at[k]
            ).start()
        own = state[OWN_ROWS, 0:32]
        edge_ns[...] = own.astype(BF16)
        edge_ew[0] = own[:, 0:8].astype(BF16)
        edge_ew[1] = own[:, 24:32].astype(BF16)
        member_cells[...] = one_hot(
            extra[OWN_ROWS, :, ASSIGN : ASSIGN + 1].reshape(8 * COLS, 1)
        )
        pick = (
            (
                lax.broadcasted_iota(jnp.int32, (BLOCKS, COLS), 0) * 2
                == lax.broadcasted_iota(jnp.int32, (BLOCKS, COLS), 1)
            )
            .astype(F32)
            .astype(BF16)
        )
        for side in range(2):
            for k in range(2):
                tokens_of = dot(pick, extra_low[4 + 4 * side + 2 * k])[:, ASSIGN : ASSIGN + 1]
                member_blocks[side, k * BLOCKS : (k + 1) * BLOCKS] = one_hot(tokens_of)
        total = partial_send[t].astype(F32)
        for k in tile_steps:
            tile_copy(0, k, partial_send.at[0], partial_recv.at[k]).wait_recv()
            total += partial_recv[k].astype(F32)
        summed_all[t] = total.astype(BF16)
        for k in tile_steps:
            tile_copy(1, k, summed_all.at[t], summed_all.at[t]).start()
        for copy in weight_copies[2:7]:
            copy.wait()
        for k in tile_steps:
            sender = tile_peer(TILE_STEPS[k], -1)
            tile_copy(1, k, summed_all.at[t], summed_all.at[sender]).wait_recv()
        summed = summed_all[...].reshape(128, C)
        tokens = embed_w[...].astype(F32) + dot(summed, pool_w[...])
        normed = rms_norm(tokens, attn_gain[...]).astype(BF16)
        keys_values[g, 0] = dot(normed, qkv_w[1]).astype(BF16)
        keys_values[g, 1] = dot(normed, qkv_w[2]).astype(BF16)
        for k in ctx_steps:
            ctx_copy(k, g).start()
        queries[...] = dot(normed, qkv_w[0])
        other = pl.ds(pl.multiple_of((1 - part) * 64, 64), 64)
        for k in reversed(ctx_steps):
            sender = ctx_peer(CTX_STEPS[k], -1)
            ctx_copy(k, sender).wait_recv()
            relay_copy(k, sender, mine).start()
        for k in reversed(ctx_steps):
            relay_copy(k, ctx_peer(CTX_STEPS[k], -1), other).wait_recv()
        send_halos(1)
        query = queries[mine].astype(BF16)
        scores = jnp.concatenate(
            [
                lax.dot_general(
                    query,
                    keys_values[i, 0],
                    (((1,), (1,)), ((), ())),
                    preferred_element_type=F32,
                )
                for i in range(ctx_size)
            ],
            axis=1,
        ) * (1.0 / math.sqrt(HDIM))
        weights = jnp.exp(scores - jnp.max(scores, axis=-1, keepdims=True))
        denominator = jnp.sum(weights, axis=-1, keepdims=True)
        weights_low = weights.astype(BF16)
        weighted = dot(
            weights_low, jnp.concatenate([keys_values[i, 1] for i in range(ctx_size)], axis=0)
        )
        attention_all[t] = (weighted / denominator).astype(BF16)
        for k in tile_steps:
            tile_copy(2, k, attention_all.at[t], attention_all.at[t]).start()
        for copy in weight_copies[7:]:
            copy.wait()
        for k in tile_steps:
            sender = tile_peer(TILE_STEPS[k], -1)
            tile_copy(2, k, attention_all.at[t], attention_all.at[sender]).wait_recv()
        for i in range(tile_size):
            attention_full[
                (i % 2) * 64 : (i % 2) * 64 + 64, (i // 2) * HDIM : (i // 2 + 1) * HDIM
            ] = attention_all[i]
        attended = tokens + dot(attention_full[...], out_w[...])
        mlp_in = rms_norm(attended, mlp_gain[...]).astype(BF16)
        hidden = jax.nn.gelu(dot(mlp_in, up_w[...])).astype(BF16)
        context = (attended + dot(hidden, down_w[...])).astype(BF16)
        returned = dot(context, return_w[...])
        returned_high = returned.astype(BF16)
        for side in range(2):
            share_send[side] = (
                dot(member_blocks[side], returned_high).reshape(2, BLOCKS, C).astype(BF16)
            )
            @pl.when(inside(MOVES[side], 1))
            def _(side=side):
                share_copy(side).start()
        context_out[...] = context
        returned_low = (returned - returned_high.astype(F32)).astype(BF16)
        take_halos(beside, 1)
        share = dot(member_cells[...], returned_high) + dot(member_cells[...], returned_low)
        share = share.reshape(8, COLS, C)
        for i in range(8):
            state[4 + i] += jnp.where(column_inside, share[i], 0.0)

    def take_shares():
        take_halos(beyond, 1)
        unpick = (
            (
                lax.broadcasted_iota(jnp.int32, (COLS, BLOCKS), 0) // 2
                == lax.broadcasted_iota(jnp.int32, (COLS, BLOCKS), 1)
            )
            .astype(F32)
            .astype(BF16)
        )
        for side in range(2):
            @pl.when(inside(MOVES[side], -1))
            def _(side=side):
                share_copy(side).wait_recv()
                first = 12 if side == 0 else 0
                for k in range(2):
                    share = jnp.where(column_inside, dot(unpick, share_recv[side, k]), 0.0)
                    state[first + 2 * k] += share
                    state[first + 2 * k + 1] += share

    def half_window(half, _):
        @pl.when(half == 0)
        def _():
            for copy in edge_copies:
                copy.wait()
            pl.semaphore_wait(barrier, heard + (ctx_size - 1) + (tile_size - 1))
            send_halos(0)
            state[OWN_ROWS, 0:32] = first_ns[:, :, 0:C].astype(F32)
            take_halos(beside, 0)
            extra_low[OWN_ROWS] = extra[OWN_ROWS].astype(BF16)
            weight_copies[0].wait()
            weight_copies[1].wait()

        @pl.when(half == 1)
        def _():
            context()

        for level in range(HALF):
            fill_taps(level, range(4 + level, 12 - level))
            if level < HALF - 1:
                advance(half, level, ((5 + level, 11 - level),), COLS)

        @pl.when(half == 0)
        def _():
            take_halos(beyond, 0)
            for copy in weight_copies[2:]:
                copy.start()
            extra_low[0:4] = extra[0:4].astype(BF16)
            extra_low[12:16] = extra[12:16].astype(BF16)

        @pl.when(half == 1)
        def _():
            take_shares()

        for level in range(HALF):
            fill_taps(level, (*range(level, 4 + level), *range(12 - level, 16 - level)))
            if level < HALF - 1:
                spans = ((1 + level, 5 + level), (11 - level, 15 - level))
                advance(half, level, spans, COLS)
            else:
                advance(half, level, ((4, 12),), 32)
        return 0

    lax.fori_loop(0, 2, half_window, 0)
    state_out[...] = state[OWN_ROWS, 0:32].astype(BF16)
    drain_halos(0)
    drain_halos(1)
    for k in tile_steps:
        tile_copy(0, k, partial_send.at[0], partial_recv.at[k]).wait_send()
        tile_copy(1, k, summed_all.at[t], summed_all.at[t]).wait_send()
        tile_copy(2, k, attention_all.at[t], attention_all.at[t]).wait_send()
    for k in ctx_steps:
        ctx_copy(k, g).wait_send()
        relay_copy(k, g, mine).wait_send()
    for side in range(2):
        @pl.when(inside(MOVES[side], 1))
        def _(side=side):
            share_copy(side).wait_send()


def local(
    syndrome_bits,
    region_assign,
    state_in,
    bit_to_candidate,
    bit_to_gate,
    conv_weight,
    gate_weight,
    gate_bias,
    pool_weight,
    region_embed,
    attn_norm_gain,
    query_weight,
    key_weight,
    value_weight,
    out_weight,
    mlp_norm_gain,
    mlp_up,
    mlp_down,
    return_weight,
):
    rows, cols = state_in.shape[0], state_in.shape[1]
    hbm = pl.BlockSpec(memory_space=pl.ANY)
    vmem = pl.BlockSpec(memory_space=pltpu.VMEM)
    dma = pltpu.SemaphoreType.DMA
    return pl.pallas_call(
        window,
        out_shape=(
            pltpu.VMEM((rows, cols, C), BF16),
            pltpu.VMEM((128, E), BF16),
        ),
        in_specs=[hbm] * 19,
        out_specs=(vmem, vmem),
        scratch_shapes=[
            pltpu.VMEM((ROUNDS, 2, 8, 32), jnp.int32),
            pltpu.VMEM((4, 16), jnp.int32),
            pltpu.VMEM((2, C), F32),
            pltpu.VMEM((2, C), F32),
            pltpu.VMEM((1, C), F32),
            pltpu.VMEM((1, E), F32),
            pltpu.VMEM((1, E), F32),
            pltpu.VMEM((ROWS, COLS, C), F32),
            pltpu.VMEM((HALF, ROWS, COLS, 3 * C), BF16),
            pltpu.VMEM((ROWS, COLS, LANES), F32),
            pltpu.VMEM((ROWS, COLS, LANES), BF16),
            pltpu.VMEM((LANES, 2 * C), F32),
            pltpu.VMEM((9, C, C), BF16),
            pltpu.VMEM((C, C), BF16),
            pltpu.VMEM((C, E), BF16),
            pltpu.VMEM((128, E), BF16),
            pltpu.VMEM((3, E, HDIM), BF16),
            pltpu.VMEM((E, E), BF16),
            pltpu.VMEM((E, 2 * E), BF16),
            pltpu.VMEM((2 * E, E), BF16),
            pltpu.VMEM((E, C), BF16),
            pltpu.VMEM((8, 32, WIDE), BF16),
            pltpu.VMEM((2, 8, 8, WIDE), BF16),
            pltpu.VMEM((2, 4, 32, WIDE), BF16),
            pltpu.VMEM((2, 8, 8, WIDE), BF16),
            pltpu.VMEM((4, 4, 8, WIDE), BF16),
            pltpu.VMEM((8, 32, C), BF16),
            pltpu.VMEM((2, 8, 8, C), BF16),
            pltpu.VMEM((2, 4, 32, C), BF16),
            pltpu.VMEM((2, 8, 8, C), BF16),
            pltpu.VMEM((4, 4, 8, C), BF16),
            pltpu.VMEM((16, 8, C), BF16),
            pltpu.VMEM((15, 8, C), BF16),
            pltpu.VMEM((16, 8, C), BF16),
            pltpu.VMEM((128, HDIM), F32),
            pltpu.VMEM((8, 2, 128, HDIM), BF16),
            pltpu.VMEM((16, 64, HDIM), BF16),
            pltpu.VMEM((128, E), BF16),
            pltpu.VMEM((8 * COLS, 128), BF16),
            pltpu.VMEM((2, 2 * BLOCKS, 128), BF16),
            pltpu.VMEM((2, 2, BLOCKS, C), BF16),
            pltpu.VMEM((2, 2, BLOCKS, C), BF16),
            dma((7,)),
            dma((11,)),
            dma((3,)),
            dma((2, 8)),
            dma((2, 8)),
            dma((3, 15)),
            dma((3, 15)),
            dma((7,)),
            dma((7,)),
            dma((7,)),
            dma((7,)),
            dma((2, 2)),
        ],
        compiler_params=pltpu.CompilerParams(
            collective_id=0, has_side_effects=True, vmem_limit_bytes=62 << 20
        ),
        name="window",
    )(
        syndrome_bits,
        region_assign,
        state_in,
        bit_to_candidate,
        bit_to_gate,
        conv_weight,
        gate_weight,
        gate_bias.reshape(1, -1),
        pool_weight,
        region_embed,
        attn_norm_gain.reshape(1, -1),
        query_weight,
        key_weight,
        value_weight,
        out_weight,
        mlp_norm_gain.reshape(1, -1),
        mlp_up,
        mlp_down,
        return_weight,
    )


def solution(mesh):
    return jax.shard_map(
        local,
        mesh=mesh,
        in_specs=(
            P(None, None, "ctx", "tile"),
            P("ctx", "tile"),
            P("ctx", "tile", None),
            P(),
            P(),
            P(),
            P(),
            P(),
            P(),
            P("ctx", None),
            P(),
            P(),
            P(),
            P(),
            P(),
            P(),
            P(),
            P(),
            P(),
        ),
        out_specs=(P("ctx", "tile", None), P("ctx", None)),
        check_vma=False,
    )
```

```python
import functools
import math

import jax
import jax.numpy as jnp
from jax import lax
from jax.experimental import pallas as pl
from jax.experimental.pallas import tpu as pltpu
from jax.sharding import PartitionSpec as P

MESH = pl.DeviceIdType.MESH
BF16 = jnp.bfloat16
F32 = jnp.float32

HEADS = 8
HDIM = 128
ROUNDS = 8
HALF = 4
C = 512
E = 1024
ROWS = 16
COLS = 40
OWN_ROWS = slice(4, 12)
LANES = 128
ASSIGN = 40

WIDE = C + LANES
BLOCKS = 24

MOVES = ((-1, 0), (1, 0), (0, -1), (0, 1), (-1, -1), (-1, 1), (1, -1), (1, 1))

TILE_STEPS = sorted(
    ((dz, dx, dc) for dz in range(4) for dx in range(2) for dc in range(2) if dz + dx + dc),
    key=lambda s: (-(min(s[0], 4 - s[0]) + s[1]), s),
)
CTX_STEPS = sorted(
    ((dx, dy) for dx in range(2) for dy in range(4) if dx + dy),
    key=lambda s: (-(2 * s[0] + min(s[1], 4 - s[1])), s),
)


def dot(left, right):
    return jnp.dot(left, right, preferred_element_type=F32)


def rms_norm(values, gain):
    return values * lax.rsqrt(jnp.mean(values * values, axis=-1, keepdims=True) + 1e-05) * gain


def window(
    syndrome_bits,
    region_assign,
    state_in,
    bit_to_candidate,
    bit_to_gate,
    conv_weight,
    gate_weight,
    gate_bias,
    pool_weight,
    region_embed,
    attn_norm_gain,
    query_weight,
    key_weight,
    value_weight,
    out_weight,
    mlp_norm_gain,
    mlp_up,
    mlp_down,
    return_weight,
    state_out,
    context_out,
    bits,
    assign_in,
    to_candidate,
    to_gate,
    bias_in,
    attn_gain,
    mlp_gain,
    state,
    taps,
    taps_beside,
    extra,
    extra_low,
    extra_beside,
    drive,
    conv_w,
    gate_w,
    pool_w,
    embed_w,
    qkv_w,
    out_w,
    up_w,
    down_w,
    return_w,
    first_ns,
    first_ew,
    first_halo_ns,
    first_halo_ew,
    first_halo_corner,
    edge_ns,
    edge_ew,
    halo_ns,
    halo_ew,
    halo_corner,
    partial_send,
    partial_recv,
    summed_all,
    queries,
    keys_values,
    attention_all,
    attention_full,
    member_cells,
    member_blocks,
    share_send,
    share_recv,
    small_sem,
    weight_sem,
    edge_sem,
    halo_send,
    halo_recv,
    tile_send,
    tile_recv,
    ctx_send,
    ctx_recv,
    relay_send,
    relay_recv,
    share_sems,
):
    g, t = lax.axis_index("ctx"), lax.axis_index("tile")
    ctx_size, tile_size = 8, 16
    head, part = t // 2, lax.rem(t, 2)

    def tile_peer(step, sign):
        dz, dx, dc = step
        z = lax.rem(t // 4 + (dz if sign > 0 else 4 - dz), 4)
        x = lax.rem(lax.rem(t // 2, 2) + dx, 2)
        core = lax.rem(t + dc, 2)
        return z * 4 + x * 2 + core

    def ctx_peer(step, sign):
        dx, dy = step
        x = lax.rem(g // 4 + dx, 2)
        y = lax.rem(g + (dy if sign > 0 else 4 - dy), 4)
        return x * 4 + y

    def inside(move, sign):
        dg, dt = move
        peer_g, peer_t = g + sign * dg, t + sign * dt
        return (peer_g >= 0) & (peer_g < ctx_size) & (peer_t >= 0) & (peer_t < tile_size)

    barrier = pltpu.get_barrier_semaphore()
    heard = jnp.int32(0)
    for move in MOVES[4:]:
        @pl.when(inside(move, 1))
        def _(move=move):
            pl.semaphore_signal(
                barrier, 1, device_id=(g + move[0], t + move[1]), device_id_type=MESH
            )
        heard += inside(move, -1).astype(jnp.int32)
    for step in CTX_STEPS:
        pl.semaphore_signal(barrier, 1, device_id=(ctx_peer(step, 1), t), device_id_type=MESH)
    for step in TILE_STEPS:
        pl.semaphore_signal(barrier, 1, device_id=(g, tile_peer(step, 1)), device_id_type=MESH)

    small_copies = [
        pltpu.make_async_copy(src, dst, small_sem.at[i])
        for i, (src, dst) in enumerate(
            (
                (syndrome_bits, bits),
                (region_assign, assign_in),
                (bit_to_candidate, to_candidate),
                (bit_to_gate, to_gate),
                (gate_bias, bias_in),
                (attn_norm_gain, attn_gain),
                (mlp_norm_gain, mlp_gain),
            )
        )
    ]
    edge_copies = [
        pltpu.make_async_copy(state_in, first_ns.at[:, :, 0:C], edge_sem.at[0]),
    ]
    head_cols = pl.ds(pl.multiple_of(head * HDIM, HDIM), HDIM)
    weight_copies = [
        pltpu.make_async_copy(src, dst, weight_sem.at[i])
        for i, (src, dst) in enumerate(
            (
                (conv_weight, conv_w),
                (gate_weight, gate_w),
                (pool_weight, pool_w),
                (region_embed, embed_w),
                (query_weight.at[:, head_cols], qkv_w.at[0]),
                (key_weight.at[:, head_cols], qkv_w.at[1]),
                (value_weight.at[:, head_cols], qkv_w.at[2]),
                (out_weight, out_w),
                (mlp_up, up_w),
                (mlp_down, down_w),
                (return_weight, return_w),
            )
        )
    ]
    for copy in small_copies + edge_copies + weight_copies[:2]:
        copy.start()

    state[...] = jnp.zeros_like(state)
    extra[...] = jnp.zeros_like(extra)
    for copy in small_copies:
        copy.wait()

    flat = bits[...].reshape(2 * ROUNDS * 8, 32).astype(F32).astype(BF16)
    source = lax.broadcasted_iota(jnp.int32, (128, 8 * LANES), 0)
    place_to = lax.broadcasted_iota(jnp.int32, (128, 8 * LANES), 1)
    target_row, target_lane = place_to // LANES, lax.rem(place_to, LANES)
    spread = (
        (lax.rem(source, 8) == target_row)
        & (target_lane < 32)
        & (lax.rem(target_lane, 16) == source // 8)
    )
    by_row = lax.dot_general(
        flat,
        spread.astype(F32).astype(BF16),
        (((0,), (0,)), ((), ())),
        preferred_element_type=F32,
    )
    block_of = (
        lax.broadcasted_iota(jnp.int32, (32, 16), 0) // 2
        == lax.broadcasted_iota(jnp.int32, (32, 16), 1)
    )
    assign_lane = (
        (lax.broadcasted_iota(jnp.int32, (16, LANES), 1) == ASSIGN).astype(F32).astype(BF16)
    )
    lane = lax.broadcasted_iota(jnp.int32, (32, LANES), 1)
    ones = ((lane == 32) | (lane == 33)).astype(F32)
    eight = lax.broadcasted_iota(jnp.int32, (8, 1), 0)

    def pack(side, top, bottom):
        keep = (eight < 4) if side == 0 else (eight >= 4)
        return jnp.where(keep, top, pltpu.roll(bottom, 4, 0)).astype(BF16)

    extra_rows = []
    for i in range(8):
        tokens_of = jnp.where(
            block_of, assign_in[i // 2 : i // 2 + 1].astype(F32), 0.0
        ).astype(BF16)
        row = by_row[:, i * LANES : (i + 1) * LANES] + dot(tokens_of, assign_lane) + ones
        extra[4 + i, 0:32] = row
        first_ns[i, :, C:WIDE] = row.astype(BF16)
        extra_rows.append(row)
    for k in range(4):
        top, bottom = extra_rows[2 * k], extra_rows[2 * k + 1]
        first_ew[0, k, :, C:WIDE] = pack(0, top[0:8], bottom[0:8])
        first_ew[1, k, :, C:WIDE] = pack(1, top[24:32], bottom[24:32])

    lane_row = lax.broadcasted_iota(jnp.int32, (LANES, 2 * C), 0)
    both = jnp.concatenate([to_candidate[...], to_gate[...]], axis=1)
    bias = jnp.concatenate([jnp.zeros_like(bias_in[...]), bias_in[...]], axis=1)
    both_high = both.astype(BF16).astype(F32)
    both_low = both - both_high
    bias_high = bias.astype(BF16).astype(F32)
    bias_low = bias - bias_high
    even_row = lax.rem(lane_row, 2) == 0
    drive[...] = jnp.where(
        lane_row < 16,
        jnp.where(even_row, both_high[0:1], both_high[1:2]),
        jnp.where(
            lane_row < 32,
            jnp.where(even_row, both_low[0:1], both_low[1:2]),
            jnp.where(
                lane_row == 32, bias_high, jnp.where(lane_row == 33, bias_low, 0.0)
            ),
        ),
    )

    column = lax.broadcasted_iota(jnp.int32, (COLS, 1), 0)
    column_inside = ~(
        ((t == 0) & (column >= 36))
        | ((t == tile_size - 1) & (column >= 32) & (column < 36))
    )
    beside_inside = ~(((t == 0) & (eight >= 4)) | ((t == tile_size - 1) & (eight < 4)))

    def halo_parts(move, half):
        dg, dt = move
        index = MOVES.index(move)
        rows = {0: slice(0, 8), -1: slice(0, 4), 1: slice(4, 8)}[dg]
        pairs = {-1: slice(0, 2), 1: slice(2, 4)}
        side = 0 if dt == -1 else 1
        ns, ew = (edge_ns, edge_ew) if half else (first_ns, first_ew)
        if dt == 0:
            return ns.at[rows], (halo_ns if half else first_halo_ns).at[index]
        if dg == 0:
            return ew.at[side], (halo_ew if half else first_halo_ew).at[side]
        return ew.at[side, pairs[dg]], (halo_corner if half else first_halo_corner).at[index - 4]

    def halo_copy(move, half):
        source, target = halo_parts(move, half)
        index = MOVES.index(move)
        return pltpu.make_async_remote_copy(
            src_ref=source,
            dst_ref=target,
            send_sem=halo_send.at[half, index],
            recv_sem=halo_recv.at[half, index],
            device_id=(g + move[0], t + move[1]),
            device_id_type=MESH,
        )

    def send_halos(half):
        for move in MOVES[2:4] + MOVES[0:2] + MOVES[4:8]:
            @pl.when(inside(move, 1))
            def _(move=move):
                halo_copy(move, half).start()

    def drain_halos(half):
        for move in MOVES:
            @pl.when(inside(move, 1))
            def _(move=move):
                halo_copy(move, half).wait_send()

    def take_halos(moves, half):
        for move in moves:
            @pl.when(inside(move, -1))
            def _(move=move):
                dg, dt = move
                first = {0: 4, -1: 12, 1: 0}[dg]
                halo_copy(move, half).wait_recv()
                _, target = halo_parts(move, half)
                if dt == 0:
                    state[first : first + 4, 0:32] = target[:, :, 0:C].astype(F32)
                    if not half:
                        extra[first : first + 4, 0:32] = target[:, :, C:WIDE].astype(F32)
                    return
                here = (eight < 4) if dt == -1 else (eight >= 4)
                for k in range(4 if dg == 0 else 2):
                    for row in range(2):
                        i = first + 2 * k + row
                        parts = [(state, slice(0, C))]
                        if not half:
                            parts.append((extra, slice(C, WIDE)))
                        for into, lanes in parts:
                            came = target[k, :, lanes].astype(F32)
                            if row:
                                came = pltpu.roll(came, 4, 0)
                            into[i, 32:40] = jnp.where(here, came, into[i, 32:40])

    beside, beyond = MOVES[2:4], MOVES[0:2] + MOVES[4:8]

    def fill_taps(level, rows):
        for i in rows:
            row = state[i]
            shifted = (pltpu.roll(row, 1, 0), row, pltpu.roll(row, COLS - 1, 0))
            for k in range(3):
                lanes = slice(k * C, (k + 1) * C)
                taps[level, i, :, lanes] = shifted[k][0:32].astype(BF16)
                taps_beside[level, i, :, lanes] = shifted[k][32:COLS].astype(BF16)

    def advance(half, level, spans, width):
        round_index = half * HALF + level
        lane = lax.broadcasted_iota(jnp.int32, (LANES, 2 * C), 0)
        chosen = ((lane < 32) & (lax.rem(lane, 16) // 2 == round_index)) | (lane >= 32)
        drive_now = jnp.where(chosen, drive[...], 0.0).astype(BF16)
        lines = sum(high - low for low, high in spans)

        def stack(read, columns):
            parts = [read(low, high) for low, high in spans]
            whole = parts[0] if len(parts) == 1 else jnp.concatenate(parts, axis=0)
            return whole.reshape(lines * columns, whole.shape[-1])

        def cells(own, halo):
            if width < COLS:
                return stack(own, 32)
            return jnp.concatenate([stack(own, 32), stack(halo, COLS - 32)], axis=0)

        flags = cells(
            lambda low, high: extra_low[low:high], lambda low, high: extra_beside[low:high]
        )
        candidate = dot(flags, drive_now[:, 0:C])
        for a in range(3):
            candidate += dot(
                cells(
                    lambda low, high: taps[level, low + a - 1 : high + a - 1],
                    lambda low, high: taps_beside[level, low + a - 1 : high + a - 1],
                ),
                conv_w[3 * a : 3 * a + 3].reshape(3 * C, C),
            )
        gate = dot(
            cells(
                lambda low, high: taps[level, low:high, :, C : 2 * C],
                lambda low, high: taps_beside[level, low:high, :, C : 2 * C],
            ),
            gate_w[...],
        ) + dot(flags, drive_now[:, C : 2 * C])
        update = 0.5 + 0.5 * jnp.tanh(0.5 * gate)
        before = cells(
            lambda low, high: state[low:high, 0:32], lambda low, high: state[low:high, 32:COLS]
        )
        after = before + update * (jnp.tanh(candidate) - before)
        own = after[0 : lines * 32].reshape(lines, 32, C)
        if width == COLS:
            halo = after[lines * 32 :].reshape(lines, COLS - 32, C)
        at = 0
        for low, high in spans:
            for i in range(low, high):
                if i < 4:
                    there = g > 0
                elif i >= 12:
                    there = g < ctx_size - 1
                else:
                    there = None
                if there is None:
                    state[i, 0:32] = own[at]
                else:
                    state[i, 0:32] = jnp.where(there, own[at], 0.0)
                if width == COLS:
                    keep = beside_inside if there is None else beside_inside & there
                    state[i, 32:COLS] = jnp.where(keep, halo[at], 0.0)
                at += 1

    def tile_copy(phase, index, source, target):
        return pltpu.make_async_remote_copy(
            src_ref=source,
            dst_ref=target,
            send_sem=tile_send.at[phase, index],
            recv_sem=tile_recv.at[phase, index],
            device_id=(g, tile_peer(TILE_STEPS[index], 1)),
            device_id_type=MESH,
        )

    mine = pl.ds(pl.multiple_of(part * 64, 64), 64)

    def ctx_copy(index, owner):
        block = keys_values.at[owner, :, mine]
        return pltpu.make_async_remote_copy(
            src_ref=block,
            dst_ref=block,
            send_sem=ctx_send.at[index],
            recv_sem=ctx_recv.at[index],
            device_id=(ctx_peer(CTX_STEPS[index], 1), t),
            device_id_type=MESH,
        )

    def relay_copy(index, owner, which):
        block = keys_values.at[owner, :, which]
        return pltpu.make_async_remote_copy(
            src_ref=block,
            dst_ref=block,
            send_sem=relay_send.at[index],
            recv_sem=relay_recv.at[index],
            device_id=(g, t + 1 - 2 * part),
            device_id_type=MESH,
        )

    def share_copy(index):
        return pltpu.make_async_remote_copy(
            src_ref=share_send.at[index],
            dst_ref=share_recv.at[index],
            send_sem=share_sems.at[0, index],
            recv_sem=share_sems.at[1, index],
            device_id=(g + MOVES[index][0], t),
            device_id_type=MESH,
        )

    tile_steps, ctx_steps = range(len(TILE_STEPS)), range(len(CTX_STEPS))
    token_lane = lax.broadcasted_iota(jnp.int32, (128, 128), 1).astype(F32)

    def one_hot(tokens):
        count = tokens.shape[0]
        lanes = lax.broadcasted_iota(jnp.int32, (count, 128), 1).astype(F32)
        return (tokens == lanes).astype(F32).astype(BF16)

    def context():
        pooled = []
        for i in range(4, 12, 2):
            pair = state[i, 0:32] + state[i + 1, 0:32]
            pooled.append(((pair + pltpu.roll(pair, 31, 0)) * 0.25).astype(BF16))
        pooled = jnp.concatenate(pooled, axis=0)
        assign = jnp.concatenate(
            [extra[i, 0:32, ASSIGN : ASSIGN + 1] for i in range(4, 12, 2)], axis=0
        )
        even = lax.rem(lax.broadcasted_iota(jnp.int32, (128, 128), 0), 2) == 0
        member = ((assign == token_lane) & even).astype(F32).astype(BF16)
        partial = lax.dot_general(
            member, pooled, (((0,), (0,)), ((), ())), preferred_element_type=F32
        )
        partial_send[...] = partial.reshape(tile_size, 8, C).astype(BF16)
        for k in tile_steps:
            tile_copy(
                0, k, partial_send.at[tile_peer(TILE_STEPS[k], 1)], partial_recv.at[k]
            ).start()
        own = state[OWN_ROWS, 0:32]
        edge_ns[...] = own.astype(BF16)
        for k in range(4):
            edge_ew[0, k] = pack(0, own[2 * k, 0:8], own[2 * k + 1, 0:8])
            edge_ew[1, k] = pack(1, own[2 * k, 24:32], own[2 * k + 1, 24:32])
        member_cells[...] = one_hot(
            extra[OWN_ROWS, :, ASSIGN : ASSIGN + 1].reshape(8 * COLS, 1)
        )
        pick = (
            (
                lax.broadcasted_iota(jnp.int32, (BLOCKS, COLS), 0) * 2
                == lax.broadcasted_iota(jnp.int32, (BLOCKS, COLS), 1)
            )
            .astype(F32)
            .astype(BF16)
        )
        for side in range(2):
            for k in range(2):
                tokens_of = dot(pick, extra[4 + 4 * side + 2 * k].astype(BF16))[:, ASSIGN : ASSIGN + 1]
                member_blocks[side, k * BLOCKS : (k + 1) * BLOCKS] = one_hot(tokens_of)
        total = partial_send[t].astype(F32)
        for k in tile_steps:
            tile_copy(0, k, partial_send.at[0], partial_recv.at[k]).wait_recv()
            total += partial_recv[k].astype(F32)
        summed_all[t] = total.astype(BF16)
        for k in tile_steps:
            tile_copy(1, k, summed_all.at[t], summed_all.at[t]).start()
        for copy in weight_copies[2:7]:
            copy.wait()
        for k in tile_steps:
            sender = tile_peer(TILE_STEPS[k], -1)
            tile_copy(1, k, summed_all.at[t], summed_all.at[sender]).wait_recv()
        summed = summed_all[...].reshape(128, C)
        tokens = embed_w[...].astype(F32) + dot(summed, pool_w[...])
        normed = rms_norm(tokens, attn_gain[...]).astype(BF16)
        keys_values[g, 0] = dot(normed, qkv_w[1]).astype(BF16)
        keys_values[g, 1] = dot(normed, qkv_w[2]).astype(BF16)
        for k in ctx_steps:
            ctx_copy(k, g).start()
        queries[...] = dot(normed, qkv_w[0])
        other = pl.ds(pl.multiple_of((1 - part) * 64, 64), 64)
        for k in reversed(ctx_steps):
            sender = ctx_peer(CTX_STEPS[k], -1)
            ctx_copy(k, sender).wait_recv()
            relay_copy(k, sender, mine).start()
        for k in reversed(ctx_steps):
            relay_copy(k, ctx_peer(CTX_STEPS[k], -1), other).wait_recv()
        send_halos(1)
        query = queries[mine].astype(BF16)
        scores = jnp.concatenate(
            [
                lax.dot_general(
                    query,
                    keys_values[i, 0],
                    (((1,), (1,)), ((), ())),
                    preferred_element_type=F32,
                )
                for i in range(ctx_size)
            ],
            axis=1,
        ) * (1.0 / math.sqrt(HDIM))
        weights = jnp.exp(scores - jnp.max(scores, axis=-1, keepdims=True))
        denominator = jnp.sum(weights, axis=-1, keepdims=True)
        weights_low = weights.astype(BF16)
        weighted = dot(
            weights_low, jnp.concatenate([keys_values[i, 1] for i in range(ctx_size)], axis=0)
        )
        attention_all[t] = (weighted / denominator).astype(BF16)
        for k in tile_steps:
            tile_copy(2, k, attention_all.at[t], attention_all.at[t]).start()
        for copy in weight_copies[7:]:
            copy.wait()
        for k in tile_steps:
            sender = tile_peer(TILE_STEPS[k], -1)
            tile_copy(2, k, attention_all.at[t], attention_all.at[sender]).wait_recv()
        for i in range(tile_size):
            attention_full[
                (i % 2) * 64 : (i % 2) * 64 + 64, (i // 2) * HDIM : (i // 2 + 1) * HDIM
            ] = attention_all[i]
        attended = tokens + dot(attention_full[...], out_w[...])
        mlp_in = rms_norm(attended, mlp_gain[...]).astype(BF16)
        hidden = jax.nn.gelu(dot(mlp_in, up_w[...])).astype(BF16)
        context = (attended + dot(hidden, down_w[...])).astype(BF16)
        returned = dot(context, return_w[...])
        returned_high = returned.astype(BF16)
        for side in range(2):
            share_send[side] = (
                dot(member_blocks[side], returned_high).reshape(2, BLOCKS, C).astype(BF16)
            )
            @pl.when(inside(MOVES[side], 1))
            def _(side=side):
                share_copy(side).start()
        context_out[...] = context
        returned_low = (returned - returned_high.astype(F32)).astype(BF16)
        take_halos(beside, 1)
        share = dot(member_cells[...], returned_high) + dot(member_cells[...], returned_low)
        share = share.reshape(8, COLS, C)
        for i in range(8):
            state[4 + i] += jnp.where(column_inside, share[i], 0.0)

    def take_shares():
        take_halos(beyond, 1)
        unpick = (
            (
                lax.broadcasted_iota(jnp.int32, (COLS, BLOCKS), 0) // 2
                == lax.broadcasted_iota(jnp.int32, (COLS, BLOCKS), 1)
            )
            .astype(F32)
            .astype(BF16)
        )
        for side in range(2):
            @pl.when(inside(MOVES[side], -1))
            def _(side=side):
                share_copy(side).wait_recv()
                first = 12 if side == 0 else 0
                for k in range(2):
                    share = jnp.where(column_inside, dot(unpick, share_recv[side, k]), 0.0)
                    state[first + 2 * k] += share
                    state[first + 2 * k + 1] += share

    def keep_extra(low, high):
        extra_low[low:high] = extra[low:high, 0:32].astype(BF16)
        extra_beside[low:high] = extra[low:high, 32:COLS].astype(BF16)

    def half_window(half, _):
        @pl.when(half == 0)
        def _():
            for copy in edge_copies:
                copy.wait()
            state[OWN_ROWS, 0:32] = first_ns[:, :, 0:C].astype(F32)
            for k in range(4):
                top, bottom = 4 + 2 * k, 5 + 2 * k
                first_ew[0, k, :, 0:C] = pack(0, state[top, 0:8], state[bottom, 0:8])
                first_ew[1, k, :, 0:C] = pack(1, state[top, 24:32], state[bottom, 24:32])
            pl.semaphore_wait(barrier, heard + (ctx_size - 1) + (tile_size - 1))
            send_halos(0)
            take_halos(beside, 0)
            keep_extra(4, 12)
            weight_copies[0].wait()
            weight_copies[1].wait()

        @pl.when(half == 1)
        def _():
            context()

        for level in range(HALF):
            fill_taps(level, range(4 + level, 12 - level))
            if level < HALF - 1:
                advance(half, level, ((5 + level, 11 - level),), COLS)

        @pl.when(half == 0)
        def _():
            take_halos(beyond, 0)
            for copy in weight_copies[2:]:
                copy.start()
            keep_extra(0, 4)
            keep_extra(12, 16)

        @pl.when(half == 1)
        def _():
            take_shares()

        for level in range(HALF):
            fill_taps(level, (*range(level, 4 + level), *range(12 - level, 16 - level)))
            if level < HALF - 1:
                spans = ((1 + level, 5 + level), (11 - level, 15 - level))
                advance(half, level, spans, COLS)
            else:
                advance(half, level, ((4, 12),), 32)
        return 0

    lax.fori_loop(0, 2, half_window, 0)
    state_out[...] = state[OWN_ROWS, 0:32].astype(BF16)
    drain_halos(0)
    drain_halos(1)
    for k in tile_steps:
        tile_copy(0, k, partial_send.at[0], partial_recv.at[k]).wait_send()
        tile_copy(1, k, summed_all.at[t], summed_all.at[t]).wait_send()
        tile_copy(2, k, attention_all.at[t], attention_all.at[t]).wait_send()
    for k in ctx_steps:
        ctx_copy(k, g).wait_send()
        relay_copy(k, g, mine).wait_send()
    for side in range(2):
        @pl.when(inside(MOVES[side], 1))
        def _(side=side):
            share_copy(side).wait_send()


def local(
    syndrome_bits,
    region_assign,
    state_in,
    bit_to_candidate,
    bit_to_gate,
    conv_weight,
    gate_weight,
    gate_bias,
    pool_weight,
    region_embed,
    attn_norm_gain,
    query_weight,
    key_weight,
    value_weight,
    out_weight,
    mlp_norm_gain,
    mlp_up,
    mlp_down,
    return_weight,
):
    rows, cols = state_in.shape[0], state_in.shape[1]
    hbm = pl.BlockSpec(memory_space=pl.ANY)
    vmem = pl.BlockSpec(memory_space=pltpu.VMEM)
    dma = pltpu.SemaphoreType.DMA
    return pl.pallas_call(
        window,
        out_shape=(
            pltpu.VMEM((rows, cols, C), BF16),
            pltpu.VMEM((128, E), BF16),
        ),
        in_specs=[hbm] * 19,
        out_specs=(vmem, vmem),
        scratch_shapes=[
            pltpu.VMEM((ROUNDS, 2, 8, 32), jnp.int32),
            pltpu.VMEM((4, 16), jnp.int32),
            pltpu.VMEM((2, C), F32),
            pltpu.VMEM((2, C), F32),
            pltpu.VMEM((1, C), F32),
            pltpu.VMEM((1, E), F32),
            pltpu.VMEM((1, E), F32),
            pltpu.VMEM((ROWS, COLS, C), F32),
            pltpu.VMEM((HALF, ROWS, 32, 3 * C), BF16),
            pltpu.VMEM((HALF, ROWS, COLS - 32, 3 * C), BF16),
            pltpu.VMEM((ROWS, COLS, LANES), F32),
            pltpu.VMEM((ROWS, 32, LANES), BF16),
            pltpu.VMEM((ROWS, COLS - 32, LANES), BF16),
            pltpu.VMEM((LANES, 2 * C), F32),
            pltpu.VMEM((9, C, C), BF16),
            pltpu.VMEM((C, C), BF16),
            pltpu.VMEM((C, E), BF16),
            pltpu.VMEM((128, E), BF16),
            pltpu.VMEM((3, E, HDIM), BF16),
            pltpu.VMEM((E, E), BF16),
            pltpu.VMEM((E, 2 * E), BF16),
            pltpu.VMEM((2 * E, E), BF16),
            pltpu.VMEM((E, C), BF16),
            pltpu.VMEM((8, 32, WIDE), BF16),
            pltpu.VMEM((2, 4, 8, WIDE), BF16),
            pltpu.VMEM((2, 4, 32, WIDE), BF16),
            pltpu.VMEM((2, 4, 8, WIDE), BF16),
            pltpu.VMEM((4, 2, 8, WIDE), BF16),
            pltpu.VMEM((8, 32, C), BF16),
            pltpu.VMEM((2, 4, 8, C), BF16),
            pltpu.VMEM((2, 4, 32, C), BF16),
            pltpu.VMEM((2, 4, 8, C), BF16),
            pltpu.VMEM((4, 2, 8, C), BF16),
            pltpu.VMEM((16, 8, C), BF16),
            pltpu.VMEM((15, 8, C), BF16),
            pltpu.VMEM((16, 8, C), BF16),
            pltpu.VMEM((128, HDIM), F32),
            pltpu.VMEM((8, 2, 128, HDIM), BF16),
            pltpu.VMEM((16, 64, HDIM), BF16),
            pltpu.VMEM((128, E), BF16),
            pltpu.VMEM((8 * COLS, 128), BF16),
            pltpu.VMEM((2, 2 * BLOCKS, 128), BF16),
            pltpu.VMEM((2, 2, BLOCKS, C), BF16),
            pltpu.VMEM((2, 2, BLOCKS, C), BF16),
            dma((7,)),
            dma((11,)),
            dma((1,)),
            dma((2, 8)),
            dma((2, 8)),
            dma((3, 15)),
            dma((3, 15)),
            dma((7,)),
            dma((7,)),
            dma((7,)),
            dma((7,)),
            dma((2, 2)),
        ],
        compiler_params=pltpu.CompilerParams(
            collective_id=0, has_side_effects=True, vmem_limit_bytes=62 << 20
        ),
        name="window",
    )(
        syndrome_bits,
        region_assign,
        state_in,
        bit_to_candidate,
        bit_to_gate,
        conv_weight,
        gate_weight,
        gate_bias.reshape(1, -1),
        pool_weight,
        region_embed,
        attn_norm_gain.reshape(1, -1),
        query_weight,
        key_weight,
        value_weight,
        out_weight,
        mlp_norm_gain.reshape(1, -1),
        mlp_up,
        mlp_down,
        return_weight,
    )


def solution(mesh):
    return jax.shard_map(
        local,
        mesh=mesh,
        in_specs=(
            P(None, None, "ctx", "tile"),
            P("ctx", "tile"),
            P("ctx", "tile", None),
            P(),
            P(),
            P(),
            P(),
            P(),
            P(),
            P("ctx", None),
            P(),
            P(),
            P(),
            P(),
            P(),
            P(),
            P(),
            P(),
            P(),
        ),
        out_specs=(P("ctx", "tile", None), P("ctx", None)),
        check_vma=False,
    )
```

```python
import functools
import math

import jax
import jax.numpy as jnp
from jax import lax
from jax.experimental import pallas as pl
from jax.experimental.pallas import tpu as pltpu
from jax.sharding import PartitionSpec as P

MESH = pl.DeviceIdType.MESH
BF16 = jnp.bfloat16
F32 = jnp.float32

HEADS = 8
HDIM = 128
ROUNDS = 8
HALF = 4
C = 512
E = 1024
ROWS = 16
COLS = 40
OWN_ROWS = slice(4, 12)
LANES = 128
ASSIGN = 40

WIDE = C + LANES
BLOCKS = 24

MOVES = ((-1, 0), (1, 0), (0, -1), (0, 1), (-1, -1), (-1, 1), (1, -1), (1, 1))

TILE_STEPS = sorted(
    ((dz, dx, dc) for dz in range(4) for dx in range(2) for dc in range(2) if dz + dx + dc),
    key=lambda s: (-(min(s[0], 4 - s[0]) + s[1]), s),
)
CTX_STEPS = sorted(
    ((dx, dy) for dx in range(2) for dy in range(4) if dx + dy),
    key=lambda s: (-(2 * s[0] + min(s[1], 4 - s[1])), s),
)


def dot(left, right):
    return jnp.dot(left, right, preferred_element_type=F32)


def rms_norm(values, gain):
    return values * lax.rsqrt(jnp.mean(values * values, axis=-1, keepdims=True) + 1e-05) * gain


def window(
    syndrome_bits,
    region_assign,
    state_in,
    bit_to_candidate,
    bit_to_gate,
    conv_weight,
    gate_weight,
    gate_bias,
    pool_weight,
    region_embed,
    attn_norm_gain,
    query_weight,
    key_weight,
    value_weight,
    out_weight,
    mlp_norm_gain,
    mlp_up,
    mlp_down,
    return_weight,
    state_out,
    context_out,
    bits,
    assign_in,
    to_candidate,
    to_gate,
    bias_in,
    attn_gain,
    mlp_gain,
    state,
    taps,
    taps_beside,
    extra,
    extra_low,
    extra_beside,
    drive,
    conv_w,
    gate_w,
    pool_w,
    embed_w,
    qkv_w,
    out_w,
    up_w,
    down_w,
    return_w,
    first_ns,
    first_ew,
    first_halo_ns,
    first_halo_ew,
    first_halo_corner,
    edge_ns,
    edge_ew,
    halo_ns,
    halo_ew,
    halo_corner,
    partial_send,
    partial_recv,
    summed_all,
    queries,
    keys_values,
    attention_all,
    attention_full,
    member_cells,
    member_blocks,
    share_send,
    share_recv,
    small_sem,
    weight_sem,
    edge_sem,
    halo_send,
    halo_recv,
    tile_send,
    tile_recv,
    ctx_send,
    ctx_recv,
    relay_send,
    relay_recv,
    share_sems,
):
    g, t = lax.axis_index("ctx"), lax.axis_index("tile")
    ctx_size, tile_size = 8, 16
    head, part = t // 2, lax.rem(t, 2)

    def tile_peer(step, sign):
        dz, dx, dc = step
        z = lax.rem(t // 4 + (dz if sign > 0 else 4 - dz), 4)
        x = lax.rem(lax.rem(t // 2, 2) + dx, 2)
        core = lax.rem(t + dc, 2)
        return z * 4 + x * 2 + core

    def ctx_peer(step, sign):
        dx, dy = step
        x = lax.rem(g // 4 + dx, 2)
        y = lax.rem(g + (dy if sign > 0 else 4 - dy), 4)
        return x * 4 + y

    def inside(move, sign):
        dg, dt = move
        peer_g, peer_t = g + sign * dg, t + sign * dt
        return (peer_g >= 0) & (peer_g < ctx_size) & (peer_t >= 0) & (peer_t < tile_size)

    barrier = pltpu.get_barrier_semaphore()
    heard = jnp.int32(0)
    for move in MOVES[4:]:
        @pl.when(inside(move, 1))
        def _(move=move):
            pl.semaphore_signal(
                barrier, 1, device_id=(g + move[0], t + move[1]), device_id_type=MESH
            )
        heard += inside(move, -1).astype(jnp.int32)
    for step in CTX_STEPS:
        pl.semaphore_signal(barrier, 1, device_id=(ctx_peer(step, 1), t), device_id_type=MESH)
    for step in TILE_STEPS:
        pl.semaphore_signal(barrier, 1, device_id=(g, tile_peer(step, 1)), device_id_type=MESH)

    small_copies = [
        pltpu.make_async_copy(src, dst, small_sem.at[i])
        for i, (src, dst) in enumerate(
            (
                (syndrome_bits, bits),
                (region_assign, assign_in),
                (bit_to_candidate, to_candidate),
                (bit_to_gate, to_gate),
                (gate_bias, bias_in),
                (attn_norm_gain, attn_gain),
                (mlp_norm_gain, mlp_gain),
            )
        )
    ]
    edge_copies = [
        pltpu.make_async_copy(state_in, first_ns.at[:, :, 0:C], edge_sem.at[0]),
    ]
    head_cols = pl.ds(pl.multiple_of(head * HDIM, HDIM), HDIM)
    weight_copies = [
        pltpu.make_async_copy(src, dst, weight_sem.at[i])
        for i, (src, dst) in enumerate(
            (
                (conv_weight, conv_w),
                (gate_weight, gate_w),
                (pool_weight, pool_w),
                (region_embed, embed_w),
                (query_weight.at[:, head_cols], qkv_w.at[0]),
                (key_weight.at[:, head_cols], qkv_w.at[1]),
                (value_weight.at[:, head_cols], qkv_w.at[2]),
                (out_weight, out_w),
                (mlp_up, up_w),
                (mlp_down, down_w),
                (return_weight, return_w),
            )
        )
    ]
    for copy in small_copies + edge_copies + weight_copies[:2]:
        copy.start()

    state[...] = jnp.zeros_like(state)
    extra[...] = jnp.zeros_like(extra)
    for copy in small_copies:
        copy.wait()

    flat = bits[...].reshape(2 * ROUNDS * 8, 32).astype(F32).astype(BF16)
    source = lax.broadcasted_iota(jnp.int32, (128, 8 * LANES), 0)
    place_to = lax.broadcasted_iota(jnp.int32, (128, 8 * LANES), 1)
    target_row, target_lane = place_to // LANES, lax.rem(place_to, LANES)
    spread = (
        (lax.rem(source, 8) == target_row)
        & (target_lane < 32)
        & (lax.rem(target_lane, 16) == source // 8)
    )
    by_row = lax.dot_general(
        flat,
        spread.astype(F32).astype(BF16),
        (((0,), (0,)), ((), ())),
        preferred_element_type=F32,
    )
    block_of = (
        lax.broadcasted_iota(jnp.int32, (32, 16), 0) // 2
        == lax.broadcasted_iota(jnp.int32, (32, 16), 1)
    )
    assign_lane = (
        (lax.broadcasted_iota(jnp.int32, (16, LANES), 1) == ASSIGN).astype(F32).astype(BF16)
    )
    lane = lax.broadcasted_iota(jnp.int32, (32, LANES), 1)
    ones = ((lane == 32) | (lane == 33)).astype(F32)
    eight = lax.broadcasted_iota(jnp.int32, (8, 1), 0)

    def pack(side, top, bottom):
        keep = (eight < 4) if side == 0 else (eight >= 4)
        return jnp.where(keep, top, pltpu.roll(bottom, 4, 0)).astype(BF16)

    extra_rows = []
    for i in range(8):
        tokens_of = jnp.where(
            block_of, assign_in[i // 2 : i // 2 + 1].astype(F32), 0.0
        ).astype(BF16)
        row = by_row[:, i * LANES : (i + 1) * LANES] + dot(tokens_of, assign_lane) + ones
        extra[4 + i, 0:32] = row
        first_ns[i, :, C:WIDE] = row.astype(BF16)
        extra_rows.append(row)
    for k in range(4):
        top, bottom = extra_rows[2 * k], extra_rows[2 * k + 1]
        first_ew[0, k, :, C:WIDE] = pack(0, top[0:8], bottom[0:8])
        first_ew[1, k, :, C:WIDE] = pack(1, top[24:32], bottom[24:32])

    lane_row = lax.broadcasted_iota(jnp.int32, (LANES, 2 * C), 0)
    both = jnp.concatenate([to_candidate[...], to_gate[...]], axis=1)
    bias = jnp.concatenate([jnp.zeros_like(bias_in[...]), bias_in[...]], axis=1)
    both_high = both.astype(BF16).astype(F32)
    both_low = both - both_high
    bias_high = bias.astype(BF16).astype(F32)
    bias_low = bias - bias_high
    even_row = lax.rem(lane_row, 2) == 0
    drive[...] = jnp.where(
        lane_row < 16,
        jnp.where(even_row, both_high[0:1], both_high[1:2]),
        jnp.where(
            lane_row < 32,
            jnp.where(even_row, both_low[0:1], both_low[1:2]),
            jnp.where(
                lane_row == 32, bias_high, jnp.where(lane_row == 33, bias_low, 0.0)
            ),
        ),
    )

    column = lax.broadcasted_iota(jnp.int32, (COLS, 1), 0)
    column_inside = ~(
        ((t == 0) & (column >= 36))
        | ((t == tile_size - 1) & (column >= 32) & (column < 36))
    )
    beside_inside = ~(((t == 0) & (eight >= 4)) | ((t == tile_size - 1) & (eight < 4)))

    def halo_parts(move, half):
        dg, dt = move
        index = MOVES.index(move)
        rows = {0: slice(0, 8), -1: slice(0, 4), 1: slice(4, 8)}[dg]
        pairs = {-1: slice(0, 2), 1: slice(2, 4)}
        side = 0 if dt == -1 else 1
        ns, ew = (edge_ns, edge_ew) if half else (first_ns, first_ew)
        if dt == 0:
            return ns.at[rows], (halo_ns if half else first_halo_ns).at[index]
        if dg == 0:
            return ew.at[side], (halo_ew if half else first_halo_ew).at[side]
        return ew.at[side, pairs[dg]], (halo_corner if half else first_halo_corner).at[index - 4]

    def halo_copy(move, half):
        source, target = halo_parts(move, half)
        index = MOVES.index(move)
        return pltpu.make_async_remote_copy(
            src_ref=source,
            dst_ref=target,
            send_sem=halo_send.at[half, index],
            recv_sem=halo_recv.at[half, index],
            device_id=(g + move[0], t + move[1]),
            device_id_type=MESH,
        )

    def send_halos(half):
        for move in MOVES[2:4] + MOVES[0:2] + MOVES[4:8]:
            @pl.when(inside(move, 1))
            def _(move=move):
                halo_copy(move, half).start()

    def drain_halos(half):
        for move in MOVES:
            @pl.when(inside(move, 1))
            def _(move=move):
                halo_copy(move, half).wait_send()

    def take_halos(moves, half):
        for move in moves:
            @pl.when(inside(move, -1))
            def _(move=move):
                dg, dt = move
                first = {0: 4, -1: 12, 1: 0}[dg]
                halo_copy(move, half).wait_recv()
                _, target = halo_parts(move, half)
                if dt == 0:
                    state[first : first + 4, 0:32] = target[:, :, 0:C].astype(F32)
                    if not half:
                        extra[first : first + 4, 0:32] = target[:, :, C:WIDE].astype(F32)
                    return
                here = (eight < 4) if dt == -1 else (eight >= 4)
                for k in range(4 if dg == 0 else 2):
                    for row in range(2):
                        i = first + 2 * k + row
                        parts = [(state, slice(0, C))]
                        if not half:
                            parts.append((extra, slice(C, WIDE)))
                        for into, lanes in parts:
                            came = target[k, :, lanes].astype(F32)
                            if row:
                                came = pltpu.roll(came, 4, 0)
                            into[i, 32:40] = jnp.where(here, came, into[i, 32:40])

    beside, beyond = MOVES[2:4], MOVES[0:2] + MOVES[4:8]

    def fill_taps(level, rows):
        for i in rows:
            row = state[i]
            shifted = (pltpu.roll(row, 1, 0), row, pltpu.roll(row, COLS - 1, 0))
            for k in range(3):
                lanes = slice(k * C, (k + 1) * C)
                taps[level, i, :, lanes] = shifted[k][0:32].astype(BF16)
                taps_beside[level, i, :, lanes] = shifted[k][32:COLS].astype(BF16)

    def advance(half, level, spans, width):
        round_index = half * HALF + level
        lane = lax.broadcasted_iota(jnp.int32, (LANES, 2 * C), 0)
        chosen = ((lane < 32) & (lax.rem(lane, 16) // 2 == round_index)) | (lane >= 32)
        drive_now = jnp.where(chosen, drive[...], 0.0).astype(BF16)
        lines = sum(high - low for low, high in spans)

        def stack(read, columns):
            parts = [read(low, high) for low, high in spans]
            whole = parts[0] if len(parts) == 1 else jnp.concatenate(parts, axis=0)
            return whole.reshape(lines * columns, whole.shape[-1])

        def cells(own, halo):
            if width < COLS:
                return stack(own, 32)
            return jnp.concatenate([stack(own, 32), stack(halo, COLS - 32)], axis=0)

        flags = cells(
            lambda low, high: extra_low[low:high], lambda low, high: extra_beside[low:high]
        )
        candidate = dot(flags, drive_now[:, 0:C])
        for a in range(3):
            candidate += dot(
                cells(
                    lambda low, high: taps[level, low + a - 1 : high + a - 1],
                    lambda low, high: taps_beside[level, low + a - 1 : high + a - 1],
                ),
                conv_w[3 * a : 3 * a + 3].reshape(3 * C, C),
            )
        gate = dot(
            cells(
                lambda low, high: taps[level, low:high, :, C : 2 * C],
                lambda low, high: taps_beside[level, low:high, :, C : 2 * C],
            ),
            gate_w[...],
        ) + dot(flags, drive_now[:, C : 2 * C])
        update = 0.5 + 0.5 * jnp.tanh(0.5 * gate)
        before = cells(
            lambda low, high: state[low:high, 0:32], lambda low, high: state[low:high, 32:COLS]
        )
        after = before + update * (jnp.tanh(candidate) - before)
        own = after[0 : lines * 32].reshape(lines, 32, C)
        if width == COLS:
            halo = after[lines * 32 :].reshape(lines, COLS - 32, C)
        at = 0
        for low, high in spans:
            for i in range(low, high):
                if i < 4:
                    there = g > 0
                elif i >= 12:
                    there = g < ctx_size - 1
                else:
                    there = None
                if there is None:
                    state[i, 0:32] = own[at]
                else:
                    state[i, 0:32] = jnp.where(there, own[at], 0.0)
                if width == COLS:
                    keep = beside_inside if there is None else beside_inside & there
                    state[i, 32:COLS] = jnp.where(keep, halo[at], 0.0)
                at += 1

    def tile_copy(phase, index, source, target):
        return pltpu.make_async_remote_copy(
            src_ref=source,
            dst_ref=target,
            send_sem=tile_send.at[phase, index],
            recv_sem=tile_recv.at[phase, index],
            device_id=(g, tile_peer(TILE_STEPS[index], 1)),
            device_id_type=MESH,
        )

    mine = pl.ds(pl.multiple_of(part * 64, 64), 64)

    def ctx_copy(index, owner):
        block = keys_values.at[owner, :, mine]
        return pltpu.make_async_remote_copy(
            src_ref=block,
            dst_ref=block,
            send_sem=ctx_send.at[index],
            recv_sem=ctx_recv.at[index],
            device_id=(ctx_peer(CTX_STEPS[index], 1), t),
            device_id_type=MESH,
        )

    def relay_copy(index, owner, which):
        block = keys_values.at[owner, :, which]
        return pltpu.make_async_remote_copy(
            src_ref=block,
            dst_ref=block,
            send_sem=relay_send.at[index],
            recv_sem=relay_recv.at[index],
            device_id=(g, t + 1 - 2 * part),
            device_id_type=MESH,
        )

    def share_copy(index):
        return pltpu.make_async_remote_copy(
            src_ref=share_send.at[index],
            dst_ref=share_recv.at[index],
            send_sem=share_sems.at[0, index],
            recv_sem=share_sems.at[1, index],
            device_id=(g + MOVES[index][0], t),
            device_id_type=MESH,
        )

    tile_steps, ctx_steps = range(len(TILE_STEPS)), range(len(CTX_STEPS))
    token_lane = lax.broadcasted_iota(jnp.int32, (128, 128), 1).astype(F32)

    def one_hot(tokens):
        count = tokens.shape[0]
        lanes = lax.broadcasted_iota(jnp.int32, (count, 128), 1).astype(F32)
        return (tokens == lanes).astype(F32).astype(BF16)

    def context():
        pooled = []
        for i in range(4, 12, 2):
            pair = state[i, 0:32] + state[i + 1, 0:32]
            pooled.append(((pair + pltpu.roll(pair, 31, 0)) * 0.25).astype(BF16))
        pooled = jnp.concatenate(pooled, axis=0)
        assign = jnp.concatenate(
            [extra[i, 0:32, ASSIGN : ASSIGN + 1] for i in range(4, 12, 2)], axis=0
        )
        even = lax.rem(lax.broadcasted_iota(jnp.int32, (128, 128), 0), 2) == 0
        member = ((assign == token_lane) & even).astype(F32).astype(BF16)
        partial = lax.dot_general(
            member, pooled, (((0,), (0,)), ((), ())), preferred_element_type=F32
        )
        partial_send[...] = partial.reshape(tile_size, 8, C).astype(BF16)
        for k in tile_steps:
            tile_copy(
                0, k, partial_send.at[tile_peer(TILE_STEPS[k], 1)], partial_recv.at[k]
            ).start()
        own = state[OWN_ROWS, 0:32]
        edge_ns[...] = own.astype(BF16)
        for k in range(4):
            edge_ew[0, k] = pack(0, own[2 * k, 0:8], own[2 * k + 1, 0:8])
            edge_ew[1, k] = pack(1, own[2 * k, 24:32], own[2 * k + 1, 24:32])
        member_cells[...] = one_hot(
            extra[OWN_ROWS, :, ASSIGN : ASSIGN + 1].reshape(8 * COLS, 1)
        )
        pick = (
            (
                lax.broadcasted_iota(jnp.int32, (BLOCKS, COLS), 0) * 2
                == lax.broadcasted_iota(jnp.int32, (BLOCKS, COLS), 1)
            )
            .astype(F32)
            .astype(BF16)
        )
        for side in range(2):
            for k in range(2):
                tokens_of = dot(pick, extra[4 + 4 * side + 2 * k].astype(BF16))[:, ASSIGN : ASSIGN + 1]
                member_blocks[side, k * BLOCKS : (k + 1) * BLOCKS] = one_hot(tokens_of)
        total = partial_send[t].astype(F32)
        for k in tile_steps:
            tile_copy(0, k, partial_send.at[0], partial_recv.at[k]).wait_recv()
            total += partial_recv[k].astype(F32)
        summed_all[t] = total.astype(BF16)
        for k in tile_steps:
            tile_copy(1, k, summed_all.at[t], summed_all.at[t]).start()
        for copy in weight_copies[2:7]:
            copy.wait()
        for k in tile_steps:
            sender = tile_peer(TILE_STEPS[k], -1)
            tile_copy(1, k, summed_all.at[t], summed_all.at[sender]).wait_recv()
        summed = summed_all[...].reshape(128, C)
        tokens = embed_w[...].astype(F32) + dot(summed, pool_w[...])
        normed = rms_norm(tokens, attn_gain[...]).astype(BF16)
        keys_values[g, 0] = dot(normed, qkv_w[1]).T.astype(BF16)
        keys_values[g, 1] = dot(normed, qkv_w[2]).astype(BF16)
        for k in ctx_steps:
            ctx_copy(k, g).start()
        queries[...] = dot(normed, qkv_w[0])
        other = pl.ds(pl.multiple_of((1 - part) * 64, 64), 64)
        for k in reversed(ctx_steps):
            sender = ctx_peer(CTX_STEPS[k], -1)
            ctx_copy(k, sender).wait_recv()
            relay_copy(k, sender, mine).start()
        for k in reversed(ctx_steps):
            relay_copy(k, ctx_peer(CTX_STEPS[k], -1), other).wait_recv()
        query = queries[mine].astype(BF16)
        scores = dot(
            query, jnp.concatenate([keys_values[i, 0] for i in range(ctx_size)], axis=1)
        ) * (1.0 / math.sqrt(HDIM))
        weights = jnp.exp(scores - jnp.max(scores, axis=-1, keepdims=True))
        denominator = jnp.sum(weights, axis=-1, keepdims=True)
        weights_low = weights.astype(BF16)
        weighted = dot(
            weights_low, jnp.concatenate([keys_values[i, 1] for i in range(ctx_size)], axis=0)
        )
        attention_all[t] = (weighted / denominator).astype(BF16)
        for k in tile_steps:
            tile_copy(2, k, attention_all.at[t], attention_all.at[t]).start()
        for copy in weight_copies[7:]:
            copy.wait()
        for k in tile_steps:
            sender = tile_peer(TILE_STEPS[k], -1)
            tile_copy(2, k, attention_all.at[t], attention_all.at[sender]).wait_recv()
        send_halos(1)
        for i in range(tile_size):
            attention_full[
                (i % 2) * 64 : (i % 2) * 64 + 64, (i // 2) * HDIM : (i // 2 + 1) * HDIM
            ] = attention_all[i]
        attended = tokens + dot(attention_full[...], out_w[...])
        mlp_in = rms_norm(attended, mlp_gain[...]).astype(BF16)
        hidden = jax.nn.gelu(dot(mlp_in, up_w[...])).astype(BF16)
        context = (attended + dot(hidden, down_w[...])).astype(BF16)
        returned = dot(context, return_w[...])
        returned_high = returned.astype(BF16)
        for side in range(2):
            share_send[side] = (
                dot(member_blocks[side], returned_high).reshape(2, BLOCKS, C).astype(BF16)
            )
            @pl.when(inside(MOVES[side], 1))
            def _(side=side):
                share_copy(side).start()
        context_out[...] = context
        returned_low = (returned - returned_high.astype(F32)).astype(BF16)
        take_halos(beside, 1)
        share = dot(member_cells[...], returned_high) + dot(member_cells[...], returned_low)
        share = share.reshape(8, COLS, C)
        for i in range(8):
            state[4 + i] += jnp.where(column_inside, share[i], 0.0)

    def take_shares():
        take_halos(beyond, 1)
        unpick = (
            (
                lax.broadcasted_iota(jnp.int32, (COLS, BLOCKS), 0) // 2
                == lax.broadcasted_iota(jnp.int32, (COLS, BLOCKS), 1)
            )
            .astype(F32)
            .astype(BF16)
        )
        for side in range(2):
            @pl.when(inside(MOVES[side], -1))
            def _(side=side):
                share_copy(side).wait_recv()
                first = 12 if side == 0 else 0
                for k in range(2):
                    share = jnp.where(column_inside, dot(unpick, share_recv[side, k]), 0.0)
                    state[first + 2 * k] += share
                    state[first + 2 * k + 1] += share

    def keep_extra(low, high):
        extra_low[low:high] = extra[low:high, 0:32].astype(BF16)
        extra_beside[low:high] = extra[low:high, 32:COLS].astype(BF16)

    def half_window(half, _):
        @pl.when(half == 0)
        def _():
            for copy in edge_copies:
                copy.wait()
            state[OWN_ROWS, 0:32] = first_ns[:, :, 0:C].astype(F32)
            for k in range(4):
                top, bottom = 4 + 2 * k, 5 + 2 * k
                first_ew[0, k, :, 0:C] = pack(0, state[top, 0:8], state[bottom, 0:8])
                first_ew[1, k, :, 0:C] = pack(1, state[top, 24:32], state[bottom, 24:32])
            pl.semaphore_wait(barrier, heard + (ctx_size - 1) + (tile_size - 1))
            send_halos(0)
            take_halos(beside, 0)
            keep_extra(4, 12)
            weight_copies[0].wait()
            weight_copies[1].wait()

        @pl.when(half == 1)
        def _():
            context()

        for level in range(HALF):
            fill_taps(level, range(4 + level, 12 - level))
            if level < HALF - 1:
                advance(half, level, ((5 + level, 11 - level),), COLS)

        @pl.when(half == 0)
        def _():
            take_halos(beyond, 0)
            for copy in weight_copies[2:]:
                copy.start()
            keep_extra(0, 4)
            keep_extra(12, 16)

        @pl.when(half == 1)
        def _():
            take_shares()

        for level in range(HALF):
            fill_taps(level, (*range(level, 4 + level), *range(12 - level, 16 - level)))
            if level < HALF - 1:
                spans = ((1 + level, 5 + level), (11 - level, 15 - level))
                advance(half, level, spans, COLS)
            else:
                advance(half, level, ((4, 12),), 32)
        return 0

    lax.fori_loop(0, 2, half_window, 0)
    state_out[...] = state[OWN_ROWS, 0:32].astype(BF16)
    drain_halos(0)
    drain_halos(1)
    for k in tile_steps:
        tile_copy(0, k, partial_send.at[0], partial_recv.at[k]).wait_send()
        tile_copy(1, k, summed_all.at[t], summed_all.at[t]).wait_send()
        tile_copy(2, k, attention_all.at[t], attention_all.at[t]).wait_send()
    for k in ctx_steps:
        ctx_copy(k, g).wait_send()
        relay_copy(k, g, mine).wait_send()
    for side in range(2):
        @pl.when(inside(MOVES[side], 1))
        def _(side=side):
            share_copy(side).wait_send()


def put_out(state_low, context, state_out, context_out, sems):
    copies = [
        pltpu.make_async_copy(state_low, state_out, sems.at[0]),
        pltpu.make_async_copy(context, context_out, sems.at[1]),
    ]
    for copy in copies:
        copy.start()
    for copy in copies:
        copy.wait()


def local(
    syndrome_bits,
    region_assign,
    state_in,
    bit_to_candidate,
    bit_to_gate,
    conv_weight,
    gate_weight,
    gate_bias,
    pool_weight,
    region_embed,
    attn_norm_gain,
    query_weight,
    key_weight,
    value_weight,
    out_weight,
    mlp_norm_gain,
    mlp_up,
    mlp_down,
    return_weight,
):
    rows, cols = state_in.shape[0], state_in.shape[1]
    hbm = pl.BlockSpec(memory_space=pl.ANY)
    vmem = pl.BlockSpec(memory_space=pltpu.VMEM)
    dma = pltpu.SemaphoreType.DMA
    state_low, context = pl.pallas_call(
        window,
        out_shape=(
            pltpu.VMEM((rows, cols, C), BF16),
            pltpu.VMEM((128, E), BF16),
        ),
        in_specs=[hbm] * 19,
        out_specs=(vmem, vmem),
        scratch_shapes=[
            pltpu.VMEM((ROUNDS, 2, 8, 32), jnp.int32),
            pltpu.VMEM((4, 16), jnp.int32),
            pltpu.VMEM((2, C), F32),
            pltpu.VMEM((2, C), F32),
            pltpu.VMEM((1, C), F32),
            pltpu.VMEM((1, E), F32),
            pltpu.VMEM((1, E), F32),
            pltpu.VMEM((ROWS, COLS, C), F32),
            pltpu.VMEM((HALF, ROWS, 32, 3 * C), BF16),
            pltpu.VMEM((HALF, ROWS, COLS - 32, 3 * C), BF16),
            pltpu.VMEM((ROWS, COLS, LANES), F32),
            pltpu.VMEM((ROWS, 32, LANES), BF16),
            pltpu.VMEM((ROWS, COLS - 32, LANES), BF16),
            pltpu.VMEM((LANES, 2 * C), F32),
            pltpu.VMEM((9, C, C), BF16),
            pltpu.VMEM((C, C), BF16),
            pltpu.VMEM((C, E), BF16),
            pltpu.VMEM((128, E), BF16),
            pltpu.VMEM((3, E, HDIM), BF16),
            pltpu.VMEM((E, E), BF16),
            pltpu.VMEM((E, 2 * E), BF16),
            pltpu.VMEM((2 * E, E), BF16),
            pltpu.VMEM((E, C), BF16),
            pltpu.VMEM((8, 32, WIDE), BF16),
            pltpu.VMEM((2, 4, 8, WIDE), BF16),
            pltpu.VMEM((2, 4, 32, WIDE), BF16),
            pltpu.VMEM((2, 4, 8, WIDE), BF16),
            pltpu.VMEM((4, 2, 8, WIDE), BF16),
            pltpu.VMEM((8, 32, C), BF16),
            pltpu.VMEM((2, 4, 8, C), BF16),
            pltpu.VMEM((2, 4, 32, C), BF16),
            pltpu.VMEM((2, 4, 8, C), BF16),
            pltpu.VMEM((4, 2, 8, C), BF16),
            pltpu.VMEM((16, 8, C), BF16),
            pltpu.VMEM((15, 8, C), BF16),
            pltpu.VMEM((16, 8, C), BF16),
            pltpu.VMEM((128, HDIM), F32),
            pltpu.VMEM((8, 2, 128, HDIM), BF16),
            pltpu.VMEM((16, 64, HDIM), BF16),
            pltpu.VMEM((128, E), BF16),
            pltpu.VMEM((8 * COLS, 128), BF16),
            pltpu.VMEM((2, 2 * BLOCKS, 128), BF16),
            pltpu.VMEM((2, 2, BLOCKS, C), BF16),
            pltpu.VMEM((2, 2, BLOCKS, C), BF16),
            dma((7,)),
            dma((11,)),
            dma((1,)),
            dma((2, 8)),
            dma((2, 8)),
            dma((3, 15)),
            dma((3, 15)),
            dma((7,)),
            dma((7,)),
            dma((7,)),
            dma((7,)),
            dma((2, 2)),
        ],
        compiler_params=pltpu.CompilerParams(
            collective_id=0, has_side_effects=True, vmem_limit_bytes=62 << 20
        ),
        name="window",
    )(
        syndrome_bits,
        region_assign,
        state_in,
        bit_to_candidate,
        bit_to_gate,
        conv_weight,
        gate_weight,
        gate_bias.reshape(1, -1),
        pool_weight,
        region_embed,
        attn_norm_gain.reshape(1, -1),
        query_weight,
        key_weight,
        value_weight,
        out_weight,
        mlp_norm_gain.reshape(1, -1),
        mlp_up,
        mlp_down,
        return_weight,
    )
    return pl.pallas_call(
        put_out,
        out_shape=(
            jax.ShapeDtypeStruct(state_low.shape, BF16),
            jax.ShapeDtypeStruct(context.shape, BF16),
        ),
        in_specs=[vmem, vmem],
        out_specs=(hbm, hbm),
        scratch_shapes=[dma((2,))],
        name="put_out",
    )(*(pltpu.with_memory_space_constraint(x, pltpu.VMEM) for x in (state_low, context)))


def solution(mesh):
    return jax.shard_map(
        local,
        mesh=mesh,
        in_specs=(
            P(None, None, "ctx", "tile"),
            P("ctx", "tile"),
            P("ctx", "tile", None),
            P(),
            P(),
            P(),
            P(),
            P(),
            P(),
            P("ctx", None),
            P(),
            P(),
            P(),
            P(),
            P(),
            P(),
            P(),
            P(),
            P(),
        ),
        out_specs=(P("ctx", "tile", None), P("ctx", None)),
        check_vma=False,
    )
```

```python
import functools
import math

import jax
import jax.numpy as jnp
from jax import lax
from jax.experimental import pallas as pl
from jax.experimental.pallas import tpu as pltpu
from jax.sharding import PartitionSpec as P

MESH = pl.DeviceIdType.MESH
BF16 = jnp.bfloat16
F32 = jnp.float32

HEADS = 8
HDIM = 128
ROUNDS = 8
HALF = 4
C = 512
E = 1024
ROWS = 16
COLS = 40
OWN_ROWS = slice(4, 12)
LANES = 128
ASSIGN = 40

WIDE = C + LANES
BLOCKS = 24

MOVES = ((-1, 0), (1, 0), (0, -1), (0, 1), (-1, -1), (-1, 1), (1, -1), (1, 1))

TILE_STEPS = sorted(
    ((dz, dx, dc) for dz in range(4) for dx in range(2) for dc in range(2) if dz + dx + dc),
    key=lambda s: (-(min(s[0], 4 - s[0]) + s[1]), s),
)
CTX_STEPS = sorted(
    ((dx, dy) for dx in range(2) for dy in range(4) if dx + dy),
    key=lambda s: (-(2 * s[0] + min(s[1], 4 - s[1])), s),
)


def dot(left, right):
    return jnp.dot(left, right, preferred_element_type=F32)


def rms_norm(values, gain):
    return values * lax.rsqrt(jnp.mean(values * values, axis=-1, keepdims=True) + 1e-05) * gain


def window(
    syndrome_bits,
    region_assign,
    state_in,
    bit_to_candidate,
    bit_to_gate,
    conv_weight,
    gate_weight,
    gate_bias,
    pool_weight,
    region_embed,
    attn_norm_gain,
    query_weight,
    key_weight,
    value_weight,
    out_weight,
    mlp_norm_gain,
    mlp_up,
    mlp_down,
    return_weight,
    state_out,
    context_out,
    bits,
    assign_in,
    to_candidate,
    to_gate,
    bias_in,
    attn_gain,
    mlp_gain,
    state,
    taps,
    taps_beside,
    extra,
    extra_low,
    extra_beside,
    drive,
    conv_w,
    gate_w,
    pool_w,
    embed_w,
    qkv_w,
    out_w,
    up_w,
    down_w,
    return_w,
    first_ns,
    first_ew,
    first_halo_ns,
    first_halo_ew,
    first_halo_corner,
    edge_ns,
    edge_ew,
    halo_ns,
    halo_ew,
    halo_corner,
    partial_send,
    partial_recv,
    summed_all,
    queries,
    keys_values,
    attention_all,
    attention_full,
    member_cells,
    member_blocks,
    share_send,
    share_recv,
    small_sem,
    weight_sem,
    edge_sem,
    halo_send,
    halo_recv,
    tile_send,
    tile_recv,
    ctx_send,
    ctx_recv,
    relay_send,
    relay_recv,
    share_sems,
):
    g, t = lax.axis_index("ctx"), lax.axis_index("tile")
    ctx_size, tile_size = 8, 16
    head, part = t // 2, lax.rem(t, 2)

    def tile_peer(step, sign):
        dz, dx, dc = step
        z = lax.rem(t // 4 + (dz if sign > 0 else 4 - dz), 4)
        x = lax.rem(lax.rem(t // 2, 2) + dx, 2)
        core = lax.rem(t + dc, 2)
        return z * 4 + x * 2 + core

    def ctx_peer(step, sign):
        dx, dy = step
        x = lax.rem(g // 4 + dx, 2)
        y = lax.rem(g + (dy if sign > 0 else 4 - dy), 4)
        return x * 4 + y

    def inside(move, sign):
        dg, dt = move
        peer_g, peer_t = g + sign * dg, t + sign * dt
        return (peer_g >= 0) & (peer_g < ctx_size) & (peer_t >= 0) & (peer_t < tile_size)

    barrier = pltpu.get_barrier_semaphore()
    heard = jnp.int32(0)
    for move in MOVES[4:]:
        @pl.when(inside(move, 1))
        def _(move=move):
            pl.semaphore_signal(
                barrier, 1, device_id=(g + move[0], t + move[1]), device_id_type=MESH
            )
        heard += inside(move, -1).astype(jnp.int32)
    for step in CTX_STEPS:
        pl.semaphore_signal(barrier, 1, device_id=(ctx_peer(step, 1), t), device_id_type=MESH)
    for step in TILE_STEPS:
        pl.semaphore_signal(barrier, 1, device_id=(g, tile_peer(step, 1)), device_id_type=MESH)

    small_copies = [
        pltpu.make_async_copy(src, dst, small_sem.at[i])
        for i, (src, dst) in enumerate(
            (
                (syndrome_bits, bits),
                (region_assign, assign_in),
                (bit_to_candidate, to_candidate),
                (bit_to_gate, to_gate),
                (gate_bias, bias_in),
                (attn_norm_gain, attn_gain),
                (mlp_norm_gain, mlp_gain),
            )
        )
    ]
    edge_copies = [
        pltpu.make_async_copy(state_in, first_ns.at[:, :, 0:C], edge_sem.at[0]),
    ]
    head_cols = pl.ds(pl.multiple_of(head * HDIM, HDIM), HDIM)
    weight_copies = [
        pltpu.make_async_copy(src, dst, weight_sem.at[i])
        for i, (src, dst) in enumerate(
            (
                (conv_weight, conv_w),
                (gate_weight, gate_w),
                (pool_weight, pool_w),
                (region_embed, embed_w),
                (query_weight.at[:, head_cols], qkv_w.at[0]),
                (key_weight.at[:, head_cols], qkv_w.at[1]),
                (value_weight.at[:, head_cols], qkv_w.at[2]),
                (out_weight, out_w),
                (mlp_up, up_w),
                (mlp_down, down_w),
                (return_weight, return_w),
            )
        )
    ]
    for copy in small_copies + edge_copies + weight_copies[:2]:
        copy.start()

    state[...] = jnp.zeros_like(state)
    extra[...] = jnp.zeros_like(extra)
    for copy in small_copies:
        copy.wait()

    flat = bits[...].reshape(2 * ROUNDS * 8, 32).astype(F32).astype(BF16)
    source = lax.broadcasted_iota(jnp.int32, (128, 8 * LANES), 0)
    place_to = lax.broadcasted_iota(jnp.int32, (128, 8 * LANES), 1)
    target_row, target_lane = place_to // LANES, lax.rem(place_to, LANES)
    spread = (
        (lax.rem(source, 8) == target_row)
        & (target_lane < 32)
        & (lax.rem(target_lane, 16) == source // 8)
    )
    by_row = lax.dot_general(
        flat,
        spread.astype(F32).astype(BF16),
        (((0,), (0,)), ((), ())),
        preferred_element_type=F32,
    )
    block_of = (
        lax.broadcasted_iota(jnp.int32, (32, 16), 0) // 2
        == lax.broadcasted_iota(jnp.int32, (32, 16), 1)
    )
    assign_lane = (
        (lax.broadcasted_iota(jnp.int32, (16, LANES), 1) == ASSIGN).astype(F32).astype(BF16)
    )
    lane = lax.broadcasted_iota(jnp.int32, (32, LANES), 1)
    ones = ((lane == 32) | (lane == 33)).astype(F32)
    eight = lax.broadcasted_iota(jnp.int32, (8, 1), 0)

    def pack(side, top, bottom):
        keep = (eight < 4) if side == 0 else (eight >= 4)
        return jnp.where(keep, top, pltpu.roll(bottom, 4, 0)).astype(BF16)

    extra_rows = []
    for i in range(8):
        tokens_of = jnp.where(
            block_of, assign_in[i // 2 : i // 2 + 1].astype(F32), 0.0
        ).astype(BF16)
        row = by_row[:, i * LANES : (i + 1) * LANES] + dot(tokens_of, assign_lane) + ones
        extra[4 + i, 0:32] = row
        first_ns[i, :, C:WIDE] = row.astype(BF16)
        extra_rows.append(row)
    for k in range(4):
        top, bottom = extra_rows[2 * k], extra_rows[2 * k + 1]
        first_ew[0, k, :, C:WIDE] = pack(0, top[0:8], bottom[0:8])
        first_ew[1, k, :, C:WIDE] = pack(1, top[24:32], bottom[24:32])

    lane_row = lax.broadcasted_iota(jnp.int32, (LANES, 2 * C), 0)
    both = jnp.concatenate([to_candidate[...], to_gate[...]], axis=1)
    bias = jnp.concatenate([jnp.zeros_like(bias_in[...]), bias_in[...]], axis=1)
    both_high = both.astype(BF16).astype(F32)
    both_low = both - both_high
    bias_high = bias.astype(BF16).astype(F32)
    bias_low = bias - bias_high
    even_row = lax.rem(lane_row, 2) == 0
    drive[...] = jnp.where(
        lane_row < 16,
        jnp.where(even_row, both_high[0:1], both_high[1:2]),
        jnp.where(
            lane_row < 32,
            jnp.where(even_row, both_low[0:1], both_low[1:2]),
            jnp.where(
                lane_row == 32, bias_high, jnp.where(lane_row == 33, bias_low, 0.0)
            ),
        ),
    )

    column = lax.broadcasted_iota(jnp.int32, (COLS, 1), 0)
    column_inside = ~(
        ((t == 0) & (column >= 36))
        | ((t == tile_size - 1) & (column >= 32) & (column < 36))
    )
    beside_inside = ~(((t == 0) & (eight >= 4)) | ((t == tile_size - 1) & (eight < 4)))

    def halo_parts(move, half):
        dg, dt = move
        index = MOVES.index(move)
        rows = {0: slice(0, 8), -1: slice(0, 4), 1: slice(4, 8)}[dg]
        pairs = {-1: slice(0, 2), 1: slice(2, 4)}
        side = 0 if dt == -1 else 1
        ns, ew = (edge_ns, edge_ew) if half else (first_ns, first_ew)
        if dt == 0:
            return ns.at[rows], (halo_ns if half else first_halo_ns).at[index]
        if dg == 0:
            return ew.at[side], (halo_ew if half else first_halo_ew).at[side]
        return ew.at[side, pairs[dg]], (halo_corner if half else first_halo_corner).at[index - 4]

    def halo_copy(move, half):
        source, target = halo_parts(move, half)
        index = MOVES.index(move)
        return pltpu.make_async_remote_copy(
            src_ref=source,
            dst_ref=target,
            send_sem=halo_send.at[half, index],
            recv_sem=halo_recv.at[half, index],
            device_id=(g + move[0], t + move[1]),
            device_id_type=MESH,
        )

    def send_halos(half):
        for move in MOVES[2:4] + MOVES[0:2] + MOVES[4:8]:
            @pl.when(inside(move, 1))
            def _(move=move):
                halo_copy(move, half).start()

    def drain_halos(half):
        for move in MOVES:
            @pl.when(inside(move, 1))
            def _(move=move):
                halo_copy(move, half).wait_send()

    def take_halos(moves, half):
        for move in moves:
            @pl.when(inside(move, -1))
            def _(move=move):
                dg, dt = move
                first = {0: 4, -1: 12, 1: 0}[dg]
                halo_copy(move, half).wait_recv()
                _, target = halo_parts(move, half)
                if dt == 0:
                    state[first : first + 4, 0:32] = target[:, :, 0:C].astype(F32)
                    if not half:
                        extra[first : first + 4, 0:32] = target[:, :, C:WIDE].astype(F32)
                    return
                here = (eight < 4) if dt == -1 else (eight >= 4)
                for k in range(4 if dg == 0 else 2):
                    for row in range(2):
                        i = first + 2 * k + row
                        parts = [(state, slice(0, C))]
                        if not half:
                            parts.append((extra, slice(C, WIDE)))
                        for into, lanes in parts:
                            came = target[k, :, lanes].astype(F32)
                            if row:
                                came = pltpu.roll(came, 4, 0)
                            into[i, 32:40] = jnp.where(here, came, into[i, 32:40])

    beside, beyond = MOVES[2:4], MOVES[0:2] + MOVES[4:8]

    def fill_taps(level, rows):
        for i in rows:
            row = state[i]
            shifted = (pltpu.roll(row, 1, 0), row, pltpu.roll(row, COLS - 1, 0))
            for k in range(3):
                lanes = slice(k * C, (k + 1) * C)
                taps[level, i, :, lanes] = shifted[k][0:32].astype(BF16)
                taps_beside[level, i, :, lanes] = shifted[k][32:COLS].astype(BF16)

    def advance(half, level, spans, width):
        round_index = half * HALF + level
        lane = lax.broadcasted_iota(jnp.int32, (LANES, 2 * C), 0)
        chosen = ((lane < 32) & (lax.rem(lane, 16) // 2 == round_index)) | (lane >= 32)
        drive_now = jnp.where(chosen, drive[...], 0.0).astype(BF16)
        lines = sum(high - low for low, high in spans)

        def stack(read, columns):
            parts = [read(low, high) for low, high in spans]
            whole = parts[0] if len(parts) == 1 else jnp.concatenate(parts, axis=0)
            return whole.reshape(lines * columns, whole.shape[-1])

        def cells(own, halo):
            if width < COLS:
                return stack(own, 32)
            return jnp.concatenate([stack(own, 32), stack(halo, COLS - 32)], axis=0)

        flags = cells(
            lambda low, high: extra_low[low:high], lambda low, high: extra_beside[low:high]
        )
        candidate = dot(flags, drive_now[:, 0:C])
        for a in range(3):
            candidate += dot(
                cells(
                    lambda low, high: taps[level, low + a - 1 : high + a - 1],
                    lambda low, high: taps_beside[level, low + a - 1 : high + a - 1],
                ),
                conv_w[3 * a : 3 * a + 3].reshape(3 * C, C),
            )
        gate = dot(
            cells(
                lambda low, high: taps[level, low:high, :, C : 2 * C],
                lambda low, high: taps_beside[level, low:high, :, C : 2 * C],
            ),
            gate_w[...],
        ) + dot(flags, drive_now[:, C : 2 * C])
        update = 0.5 + 0.5 * jnp.tanh(0.5 * gate)
        before = cells(
            lambda low, high: state[low:high, 0:32], lambda low, high: state[low:high, 32:COLS]
        )
        after = before + update * (jnp.tanh(candidate) - before)
        own = after[0 : lines * 32].reshape(lines, 32, C)
        if width == COLS:
            halo = after[lines * 32 :].reshape(lines, COLS - 32, C)
        at = 0
        for low, high in spans:
            for i in range(low, high):
                if i < 4:
                    there = g > 0
                elif i >= 12:
                    there = g < ctx_size - 1
                else:
                    there = None
                if there is None:
                    state[i, 0:32] = own[at]
                else:
                    state[i, 0:32] = jnp.where(there, own[at], 0.0)
                if width == COLS:
                    keep = beside_inside if there is None else beside_inside & there
                    state[i, 32:COLS] = jnp.where(keep, halo[at], 0.0)
                at += 1

    def tile_copy(phase, index, source, target):
        return pltpu.make_async_remote_copy(
            src_ref=source,
            dst_ref=target,
            send_sem=tile_send.at[phase, index],
            recv_sem=tile_recv.at[phase, index],
            device_id=(g, tile_peer(TILE_STEPS[index], 1)),
            device_id_type=MESH,
        )

    mine = pl.ds(pl.multiple_of(part * 64, 64), 64)

    def ctx_copy(index, owner):
        block = keys_values.at[owner, :, mine]
        return pltpu.make_async_remote_copy(
            src_ref=block,
            dst_ref=block,
            send_sem=ctx_send.at[index],
            recv_sem=ctx_recv.at[index],
            device_id=(ctx_peer(CTX_STEPS[index], 1), t),
            device_id_type=MESH,
        )

    def relay_copy(index, owner, which):
        block = keys_values.at[owner, :, which]
        return pltpu.make_async_remote_copy(
            src_ref=block,
            dst_ref=block,
            send_sem=relay_send.at[index],
            recv_sem=relay_recv.at[index],
            device_id=(g, t + 1 - 2 * part),
            device_id_type=MESH,
        )

    def share_copy(index):
        return pltpu.make_async_remote_copy(
            src_ref=share_send.at[index],
            dst_ref=share_recv.at[index],
            send_sem=share_sems.at[0, index],
            recv_sem=share_sems.at[1, index],
            device_id=(g + MOVES[index][0], t),
            device_id_type=MESH,
        )

    tile_steps, ctx_steps = range(len(TILE_STEPS)), range(len(CTX_STEPS))
    token_lane = lax.broadcasted_iota(jnp.int32, (128, 128), 1).astype(F32)

    def one_hot(tokens):
        count = tokens.shape[0]
        lanes = lax.broadcasted_iota(jnp.int32, (count, 128), 1).astype(F32)
        return (tokens == lanes).astype(F32).astype(BF16)

    def context():
        pooled = []
        for i in range(4, 12, 2):
            pair = state[i, 0:32] + state[i + 1, 0:32]
            pooled.append(((pair + pltpu.roll(pair, 31, 0)) * 0.25).astype(BF16))
        pooled = jnp.concatenate(pooled, axis=0)
        assign = jnp.concatenate(
            [extra[i, 0:32, ASSIGN : ASSIGN + 1] for i in range(4, 12, 2)], axis=0
        )
        even = lax.rem(lax.broadcasted_iota(jnp.int32, (128, 128), 0), 2) == 0
        member = ((assign == token_lane) & even).astype(F32).astype(BF16)
        partial = lax.dot_general(
            member, pooled, (((0,), (0,)), ((), ())), preferred_element_type=F32
        )
        partial_send[...] = partial.reshape(tile_size, 8, C).astype(BF16)
        for k in tile_steps:
            tile_copy(
                0, k, partial_send.at[tile_peer(TILE_STEPS[k], 1)], partial_recv.at[k]
            ).start()
        own = state[OWN_ROWS, 0:32]
        edge_ns[...] = own.astype(BF16)
        for k in range(4):
            edge_ew[0, k] = pack(0, own[2 * k, 0:8], own[2 * k + 1, 0:8])
            edge_ew[1, k] = pack(1, own[2 * k, 24:32], own[2 * k + 1, 24:32])
        member_cells[...] = one_hot(
            extra[OWN_ROWS, :, ASSIGN : ASSIGN + 1].reshape(8 * COLS, 1)
        )
        pick = (
            (
                lax.broadcasted_iota(jnp.int32, (BLOCKS, COLS), 0) * 2
                == lax.broadcasted_iota(jnp.int32, (BLOCKS, COLS), 1)
            )
            .astype(F32)
            .astype(BF16)
        )
        for side in range(2):
            for k in range(2):
                tokens_of = dot(pick, extra[4 + 4 * side + 2 * k].astype(BF16))[:, ASSIGN : ASSIGN + 1]
                member_blocks[side, k * BLOCKS : (k + 1) * BLOCKS] = one_hot(tokens_of)
        total = partial_send[t].astype(F32)
        for k in tile_steps:
            tile_copy(0, k, partial_send.at[0], partial_recv.at[k]).wait_recv()
            total += partial_recv[k].astype(F32)
        summed_all[t] = total.astype(BF16)
        for k in tile_steps:
            tile_copy(1, k, summed_all.at[t], summed_all.at[t]).start()
        for copy in weight_copies[2:7]:
            copy.wait()
        for k in tile_steps:
            sender = tile_peer(TILE_STEPS[k], -1)
            tile_copy(1, k, summed_all.at[t], summed_all.at[sender]).wait_recv()
        summed = summed_all[...].reshape(128, C)
        tokens = embed_w[...].astype(F32) + dot(summed, pool_w[...])
        normed = rms_norm(tokens, attn_gain[...]).astype(BF16)
        keys_values[g, 0] = dot(normed, qkv_w[1]).T.astype(BF16)
        keys_values[g, 1] = dot(normed, qkv_w[2]).astype(BF16)
        for k in ctx_steps:
            ctx_copy(k, g).start()
        queries[...] = dot(normed, qkv_w[0])
        other = pl.ds(pl.multiple_of((1 - part) * 64, 64), 64)
        for k in reversed(ctx_steps):
            sender = ctx_peer(CTX_STEPS[k], -1)
            ctx_copy(k, sender).wait_recv()
            relay_copy(k, sender, mine).start()
        for k in reversed(ctx_steps):
            relay_copy(k, ctx_peer(CTX_STEPS[k], -1), other).wait_recv()
        query = queries[mine].astype(BF16)
        scores = dot(
            query, jnp.concatenate([keys_values[i, 0] for i in range(ctx_size)], axis=1)
        ) * (1.0 / math.sqrt(HDIM))
        weights = jnp.exp(scores - jnp.max(scores, axis=-1, keepdims=True))
        denominator = jnp.sum(weights, axis=-1, keepdims=True)
        weights_low = weights.astype(BF16)
        weighted = dot(
            weights_low, jnp.concatenate([keys_values[i, 1] for i in range(ctx_size)], axis=0)
        )
        attention_all[t] = (weighted / denominator).astype(BF16)
        for k in tile_steps:
            tile_copy(2, k, attention_all.at[t], attention_all.at[t]).start()
        for copy in weight_copies[7:]:
            copy.wait()
        for k in tile_steps:
            sender = tile_peer(TILE_STEPS[k], -1)
            tile_copy(2, k, attention_all.at[t], attention_all.at[sender]).wait_recv()
        send_halos(1)
        for i in range(tile_size):
            attention_full[
                (i % 2) * 64 : (i % 2) * 64 + 64, (i // 2) * HDIM : (i // 2 + 1) * HDIM
            ] = attention_all[i]
        attended = tokens + dot(attention_full[...], out_w[...])
        mlp_in = rms_norm(attended, mlp_gain[...]).astype(BF16)
        hidden = jax.nn.gelu(dot(mlp_in, up_w[...])).astype(BF16)
        context = (attended + dot(hidden, down_w[...])).astype(BF16)
        returned = dot(context, return_w[...])
        returned_high = returned.astype(BF16)
        for side in range(2):
            share_send[side] = (
                dot(member_blocks[side], returned_high).reshape(2, BLOCKS, C).astype(BF16)
            )
            @pl.when(inside(MOVES[side], 1))
            def _(side=side):
                share_copy(side).start()
        context_out[...] = context
        returned_low = (returned - returned_high.astype(F32)).astype(BF16)
        take_halos(beside, 1)
        share = dot(member_cells[...], returned_high) + dot(member_cells[...], returned_low)
        share = share.reshape(8, COLS, C)
        for i in range(8):
            state[4 + i] += jnp.where(column_inside, share[i], 0.0)

    def take_shares():
        take_halos(beyond, 1)
        unpick = (
            (
                lax.broadcasted_iota(jnp.int32, (COLS, BLOCKS), 0) // 2
                == lax.broadcasted_iota(jnp.int32, (COLS, BLOCKS), 1)
            )
            .astype(F32)
            .astype(BF16)
        )
        for side in range(2):
            @pl.when(inside(MOVES[side], -1))
            def _(side=side):
                share_copy(side).wait_recv()
                first = 12 if side == 0 else 0
                for k in range(2):
                    share = jnp.where(column_inside, dot(unpick, share_recv[side, k]), 0.0)
                    state[first + 2 * k] += share
                    state[first + 2 * k + 1] += share

    def keep_extra(low, high):
        extra_low[low:high] = extra[low:high, 0:32].astype(BF16)
        extra_beside[low:high] = extra[low:high, 32:COLS].astype(BF16)

    def half_window(half, _):
        @pl.when(half == 0)
        def _():
            for copy in edge_copies:
                copy.wait()
            state[OWN_ROWS, 0:32] = first_ns[:, :, 0:C].astype(F32)
            for k in range(4):
                top, bottom = 4 + 2 * k, 5 + 2 * k
                first_ew[0, k, :, 0:C] = pack(0, state[top, 0:8], state[bottom, 0:8])
                first_ew[1, k, :, 0:C] = pack(1, state[top, 24:32], state[bottom, 24:32])
            pl.semaphore_wait(barrier, heard + (ctx_size - 1) + (tile_size - 1))
            send_halos(0)
            take_halos(beside, 0)
            keep_extra(4, 12)
            weight_copies[0].wait()
            weight_copies[1].wait()

        @pl.when(half == 1)
        def _():
            context()

        for level in range(HALF):
            fill_taps(level, range(4 + level, 12 - level))
            if level < HALF - 1:
                advance(half, level, ((5 + level, 11 - level),), COLS)

        @pl.when(half == 0)
        def _():
            take_halos(beyond, 0)
            keep_extra(0, 4)
            keep_extra(12, 16)

        @pl.when(half == 1)
        def _():
            take_shares()

        @pl.when(half == 0)
        def _():
            for copy in weight_copies[2:]:
                copy.start()

        for level in range(HALF):
            fill_taps(level, (*range(level, 4 + level), *range(12 - level, 16 - level)))
            if level < HALF - 1:
                spans = ((1 + level, 5 + level), (11 - level, 15 - level))
                advance(half, level, spans, COLS)
            else:
                advance(half, level, ((4, 12),), 32)
        return 0

    lax.fori_loop(0, 2, half_window, 0)
    state_out[...] = state[OWN_ROWS, 0:32].astype(BF16)
    drain_halos(0)
    drain_halos(1)
    for k in tile_steps:
        tile_copy(0, k, partial_send.at[0], partial_recv.at[k]).wait_send()
        tile_copy(1, k, summed_all.at[t], summed_all.at[t]).wait_send()
        tile_copy(2, k, attention_all.at[t], attention_all.at[t]).wait_send()
    for k in ctx_steps:
        ctx_copy(k, g).wait_send()
        relay_copy(k, g, mine).wait_send()
    for side in range(2):
        @pl.when(inside(MOVES[side], 1))
        def _(side=side):
            share_copy(side).wait_send()


def put_out(state_low, context, state_out, context_out, sems):
    copies = [
        pltpu.make_async_copy(state_low, state_out, sems.at[0]),
        pltpu.make_async_copy(context, context_out, sems.at[1]),
    ]
    for copy in copies:
        copy.start()
    for copy in copies:
        copy.wait()


def local(
    syndrome_bits,
    region_assign,
    state_in,
    bit_to_candidate,
    bit_to_gate,
    conv_weight,
    gate_weight,
    gate_bias,
    pool_weight,
    region_embed,
    attn_norm_gain,
    query_weight,
    key_weight,
    value_weight,
    out_weight,
    mlp_norm_gain,
    mlp_up,
    mlp_down,
    return_weight,
):
    rows, cols = state_in.shape[0], state_in.shape[1]
    hbm = pl.BlockSpec(memory_space=pl.ANY)
    vmem = pl.BlockSpec(memory_space=pltpu.VMEM)
    dma = pltpu.SemaphoreType.DMA
    state_low, context = pl.pallas_call(
        window,
        out_shape=(
            pltpu.VMEM((rows, cols, C), BF16),
            pltpu.VMEM((128, E), BF16),
        ),
        in_specs=[hbm] * 19,
        out_specs=(vmem, vmem),
        scratch_shapes=[
            pltpu.VMEM((ROUNDS, 2, 8, 32), jnp.int32),
            pltpu.VMEM((4, 16), jnp.int32),
            pltpu.VMEM((2, C), F32),
            pltpu.VMEM((2, C), F32),
            pltpu.VMEM((1, C), F32),
            pltpu.VMEM((1, E), F32),
            pltpu.VMEM((1, E), F32),
            pltpu.VMEM((ROWS, COLS, C), F32),
            pltpu.VMEM((HALF, ROWS, 32, 3 * C), BF16),
            pltpu.VMEM((HALF, ROWS, COLS - 32, 3 * C), BF16),
            pltpu.VMEM((ROWS, COLS, LANES), F32),
            pltpu.VMEM((ROWS, 32, LANES), BF16),
            pltpu.VMEM((ROWS, COLS - 32, LANES), BF16),
            pltpu.VMEM((LANES, 2 * C), F32),
            pltpu.VMEM((9, C, C), BF16),
            pltpu.VMEM((C, C), BF16),
            pltpu.VMEM((C, E), BF16),
            pltpu.VMEM((128, E), BF16),
            pltpu.VMEM((3, E, HDIM), BF16),
            pltpu.VMEM((E, E), BF16),
            pltpu.VMEM((E, 2 * E), BF16),
            pltpu.VMEM((2 * E, E), BF16),
            pltpu.VMEM((E, C), BF16),
            pltpu.VMEM((8, 32, WIDE), BF16),
            pltpu.VMEM((2, 4, 8, WIDE), BF16),
            pltpu.VMEM((2, 4, 32, WIDE), BF16),
            pltpu.VMEM((2, 4, 8, WIDE), BF16),
            pltpu.VMEM((4, 2, 8, WIDE), BF16),
            pltpu.VMEM((8, 32, C), BF16),
            pltpu.VMEM((2, 4, 8, C), BF16),
            pltpu.VMEM((2, 4, 32, C), BF16),
            pltpu.VMEM((2, 4, 8, C), BF16),
            pltpu.VMEM((4, 2, 8, C), BF16),
            pltpu.VMEM((16, 8, C), BF16),
            pltpu.VMEM((15, 8, C), BF16),
            pltpu.VMEM((16, 8, C), BF16),
            pltpu.VMEM((128, HDIM), F32),
            pltpu.VMEM((8, 2, 128, HDIM), BF16),
            pltpu.VMEM((16, 64, HDIM), BF16),
            pltpu.VMEM((128, E), BF16),
            pltpu.VMEM((8 * COLS, 128), BF16),
            pltpu.VMEM((2, 2 * BLOCKS, 128), BF16),
            pltpu.VMEM((2, 2, BLOCKS, C), BF16),
            pltpu.VMEM((2, 2, BLOCKS, C), BF16),
            dma((7,)),
            dma((11,)),
            dma((1,)),
            dma((2, 8)),
            dma((2, 8)),
            dma((3, 15)),
            dma((3, 15)),
            dma((7,)),
            dma((7,)),
            dma((7,)),
            dma((7,)),
            dma((2, 2)),
        ],
        compiler_params=pltpu.CompilerParams(
            collective_id=0, has_side_effects=True, vmem_limit_bytes=62 << 20
        ),
        name="window",
    )(
        syndrome_bits,
        region_assign,
        state_in,
        bit_to_candidate,
        bit_to_gate,
        conv_weight,
        gate_weight,
        gate_bias.reshape(1, -1),
        pool_weight,
        region_embed,
        attn_norm_gain.reshape(1, -1),
        query_weight,
        key_weight,
        value_weight,
        out_weight,
        mlp_norm_gain.reshape(1, -1),
        mlp_up,
        mlp_down,
        return_weight,
    )
    return pl.pallas_call(
        put_out,
        out_shape=(
            jax.ShapeDtypeStruct(state_low.shape, BF16),
            jax.ShapeDtypeStruct(context.shape, BF16),
        ),
        in_specs=[vmem, vmem],
        out_specs=(hbm, hbm),
        scratch_shapes=[dma((2,))],
        name="put_out",
    )(*(pltpu.with_memory_space_constraint(x, pltpu.VMEM) for x in (state_low, context)))


def solution(mesh):
    return jax.shard_map(
        local,
        mesh=mesh,
        in_specs=(
            P(None, None, "ctx", "tile"),
            P("ctx", "tile"),
            P("ctx", "tile", None),
            P(),
            P(),
            P(),
            P(),
            P(),
            P(),
            P("ctx", None),
            P(),
            P(),
            P(),
            P(),
            P(),
            P(),
            P(),
            P(),
            P(),
        ),
        out_specs=(P("ctx", "tile", None), P("ctx", None)),
        check_vma=False,
    )
```
